512 devices in a mesh: segment: 4 (over x), tx: 8 (over y, z_hi), ty: 16 (over z_lo, core).
Axes of the slice: x: 4, y: 4, z: 16 (z_hi: 2, z_lo: 8; z = z_hi * 8 + z_lo), core: 2. Of those that a mesh axis runs over, the one named last changes fastest.
Arguments:
- act_in: bfloat16 [4, 128, 1024, 128], P('segment', 'tx', 'ty'), may hold values from -6 to 6
- partner_in: bfloat16 [4, 128, 1024, 128], P('segment', 'tx', 'ty'), may hold values from -6 to 6
- stashed: bfloat16 [4, 128, 1024, 128], P('segment', 'tx', 'ty'), may hold values from -6 to 6
- grad_in: bfloat16 [4, 128, 1024, 128], P('segment', 'tx', 'ty'), may hold values from -6 to 6
- down_weights: bfloat16 [4, 3, 3, 128, 192], P('segment'), may hold values from -0.1875 to 0.1875
- up_weights: bfloat16 [4, 3, 3, 192, 128], P('segment'), may hold values from -0.15625 to 0.15625
- coarse: bfloat16 [8192, 128], P(('tx', 'ty')), may hold values from -6 to 6
- nest_owner: int32 [8192, 1], P(('tx', 'ty')), may hold values from 0 to 15; in each aligned block of 64 rows (0 to 63, 64 to 127, ...) at most 8 rows name the same one
- nest_cell: int32 [8192], P(('tx', 'ty')), may hold values from 0 to 63
- land_weight: int32 [32, 256], P('tx', 'ty'), may hold values from 1 to 4
Outputs:
- act_out: bfloat16 [4, 128, 1024, 128], P('segment', 'tx', 'ty')
- grad_out: bfloat16 [4, 128, 1024, 128], P('segment', 'tx', 'ty')
- partner_out: bfloat16 [4, 128, 1024, 128], P('segment', 'tx', 'ty')
- down_grads: float32 [4, 221184], P('segment', ('tx', 'ty'))
- up_grads: float32 [4, 221184], P('segment', ('tx', 'ty'))
The draws below stay inside these ranges and needn't reach their ends.
Inputs may be any that keep to these rules, and one draw needn't show every extreme that they name: `nest_owner`: within the rows of one device (aligned blocks of 64 rows) no owner is named more than 8 times, a bound that some block reaches; every owner is named by some row.
All inputs are finite; a program needn't handle non-finite values.
Results may differ from the reference program's by a relative error of at most 0.0085.
Values may be sent and summed in bfloat16 or wider, within the bound.
A program may use at most 64 MiB of HBM per device.

```python
import math
import jax
import jax.numpy as jnp
import numpy as np
from jax import lax

C = 128
C2 = 192
HT = 16
WT = 64
CELLS_C = 64
CAP = 8
NH = 128
NW = 1024
N_SEGMENT = 4
N_TX = 8
N_TY = 16


def plant(entries, stream_key, low, high):
    spot = [jax.random.randint(jax.random.fold_in(stream_key, axis), (), 0, length) for axis, length in enumerate(entries.shape)]
    longest = entries.shape.index(max(entries.shape))
    neighbour = spot[:longest] + [(spot[longest] + 1) % entries.shape[longest]] + spot[longest + 1:]
    return entries.at[tuple(spot)].set(low).at[tuple(neighbour)].set(high)


def levels(key, dims, cuts, low, high):
    def one(position, shards_of):
        heights = jax.random.uniform(jax.random.fold_in(jax.random.fold_in(key, 6), position), (shards_of,), jnp.float32, low / len(cuts), high / len(cuts))
        return jnp.repeat(jnp.exp(heights), dims[position] // shards_of).reshape((-1,) + (1,) * (len(dims) - position - 1))

    factor_of = one(*cuts[0])
    for cut in cuts[1:]:
        factor_of = factor_of * one(*cut)
    return factor_of


def assign_block(rng, own, number, rows, amount, top, bound, skew):
    ranking = jax.random.permutation(rng, amount)
    crowded, usual = load_shares(amount, rows * top, bound, skew, True), load_shares(amount, rows * top, bound, skew, False)
    places = jnp.arange(amount)

    def named(sizes, offset_by):
        used = int((sizes > 0).sum())
        fixed = max(1, used // 4)
        shifted = fixed + (places - fixed + offset_by * (used - fixed)) % max(1, amount - fixed)
        return jnp.zeros((amount,), jnp.int32).at[ranking[jnp.where(places < fixed, places, shifted)]].set(jnp.asarray(sizes, jnp.int32))

    sizes = jnp.where(number % 4 == 0, named(crowded, number // 4), named(usual, number - number // 4 - 1))
    mixed = jax.random.permutation(jax.random.fold_in(own, 3), amount)
    source_of, sink = mixed[0:amount // 2 * 2:2], mixed[1:amount // 2 * 2:2]
    room = jnp.minimum(sizes[source_of] - 1, bound - sizes[sink]) // 2
    room = jnp.where((source_of == ranking[0]) | (sink == ranking[0]) | (sizes[sink] == 0), 0, jnp.maximum(room, 0))
    shifted = jax.random.randint(jax.random.fold_in(own, 4), (amount // 2,), 0, 1 << 20) % (room + 1)
    sizes = sizes.at[source_of].add(-shifted).at[sink].add(shifted)
    members = jnp.searchsorted(jnp.cumsum(sizes), jnp.arange(rows * top), side="right").astype(jnp.int32)
    grid = members.reshape(top, rows).T
    grid = grid[jax.random.permutation(jax.random.fold_in(own, 1), rows)]
    offset_by = jax.random.randint(jax.random.fold_in(own, 2), (rows, 1), 0, top)
    return jnp.take_along_axis(grid, (jnp.arange(top)[None, :] + offset_by) % top, axis=1)


def load_shares(number_of, total, bound, slope, full):
    weights = [(1 << 20) // math.isqrt(rank ** slope) + 1 for rank in range(1, number_of + 1)]
    largest = bound if full else min(bound, max(-(-total // number_of), total * weights[0] // sum(weights)))
    least = 1 if total - largest >= number_of - 1 else 0
    holding, spare = [largest] + [least] * (number_of - 1), total - largest - least * (number_of - 1)
    while spare > 0:
        movable = [i for i in range(1, number_of) if holding[i] < largest] or [i for i in range(1, number_of) if holding[i] < bound]
        pool, left = sum([weights[i] for i in movable]), spare
        for i in movable:
            addition = min(bound - holding[i], max(1, left * weights[i] // pool), spare)
            holding[i] = holding[i] + addition
            spare = spare - addition
    return np.array(holding)


def gaussian(own_key, shape, width, most, cuts=(), kind=jnp.bfloat16):
    values = jax.random.normal(own_key, shape, jnp.float32) * width
    if len(cuts) > 0:
        values = levels(own_key, shape, cuts, -0.22, 0.18) * values
    return jnp.clip(values, min=-most, max=most).astype(kind)


def setup_inputs(seed: int = 0) -> dict:
    key_list = jax.random.split(jax.random.key(seed), 11)
    act_in = gaussian(key_list[0], (N_SEGMENT, NH, NW, C), 1.0, 6.0, ((0, 4), (1, 8), (2, 16)))
    partner_in = gaussian(key_list[1], (N_SEGMENT, NH, NW, C), 1.0, 6.0, ((0, 4), (1, 8), (2, 16)))
    stashed = gaussian(key_list[2], (N_SEGMENT, NH, NW, C), 1.0, 6.0, ((0, 4), (1, 8), (2, 16)))
    grad_in = gaussian(key_list[3], (N_SEGMENT, NH, NW, C), 1.0, 6.0, ((0, 4), (1, 8), (2, 16)))
    down_weights = gaussian(key_list[4], (N_SEGMENT, 3, 3, C, C2), (9 * C) ** -0.5, 0.1875, ((0, 4),))
    up_weights = gaussian(key_list[5], (N_SEGMENT, 3, 3, C2, C), (9 * C2) ** -0.5, 0.15625, ((0, 4),))
    coarse = gaussian(key_list[6], (N_TX * N_TY * CELLS_C, C), 1.0, 6.0, ((0, 128),))
    nest_owner_keys = jax.random.split(jax.random.fold_in(key_list[7], 1), (N_TX * N_TY * CELLS_C) // CELLS_C)
    nest_owner_turns = jax.random.permutation(jax.random.fold_in(key_list[7], 3), (N_TX * N_TY * CELLS_C) // CELLS_C)
    nest_owner = jax.vmap(lambda own, number: assign_block(jax.random.fold_in(key_list[7], 2), own, number, CELLS_C, N_TY, 1, CAP, 2))(nest_owner_keys, nest_owner_turns).reshape((N_TX * N_TY * CELLS_C, 1))
    nest_cell = plant(jax.random.randint(key_list[8], (N_TX * N_TY * CELLS_C,), 0, CELLS_C), jax.random.fold_in(key_list[8], 1), 0, CELLS_C - 1).astype(jnp.int32)
    land_weight = plant(jax.random.randint(key_list[9], (NH // 4, NW // 4), 1, 5), jax.random.fold_in(key_list[9], 1), 1, 4).astype(jnp.int32)
    return dict(act_in=act_in, partner_in=partner_in, stashed=stashed, grad_in=grad_in, down_weights=down_weights, up_weights=up_weights, coarse=coarse, nest_owner=nest_owner, nest_cell=nest_cell, land_weight=land_weight)


def convolve(inputs, kernel, stride, padding, dilation):
    result = lax.conv_general_dilated(inputs[None], kernel, (stride, stride), padding, lhs_dilation=(dilation, dilation), dimension_numbers=('NHWC', 'HWIO', 'NHWC'), preferred_element_type=jnp.float32)
    return result[0]

def flipped(kernel):
    return jnp.transpose(kernel[::-1, ::-1], (0, 1, 3, 2))

def enlarge(values, factor):
    return jnp.repeat(jnp.repeat(values, factor, axis=0), factor, axis=1)

def pooled(values):
    height, breadth, channels = values.shape
    return values.reshape(height // 2, 2, breadth // 2, 2, channels).sum(axis=(1, 3))

def silu_slope(preact):
    logistic = jax.nn.sigmoid(preact)
    return logistic * (1.0 + preact * (1.0 - logistic))

def kernel_grad(padded, cotangent, stride):
    height, breadth, channels = cotangent.shape
    flat_grad = cotangent.reshape(height * breadth, channels)
    pieces = []
    for row_tap in range(3):
        for col_tap in range(3):
            window = padded[row_tap:row_tap + stride * (height - 1) + 1:stride, col_tap:col_tap + stride * (breadth - 1) + 1:stride]
            window = window.reshape(height * breadth, window.shape[-1])
            pieces.append(lax.dot_general(window, flat_grad, (((0,), (0,)), ((), ())), preferred_element_type=jnp.float32))
    return jnp.stack(pieces).reshape(-1)

def lower_parts(block_cells, down_kernel):
    pre_down = convolve(block_cells, down_kernel, 2, ((1, 1), (1, 1)), 1)
    reduced = jax.nn.silu(pre_down).astype(jnp.bfloat16)
    return (pre_down, enlarge(reduced, 2))

def reference(act_in, partner_in, stashed, grad_in, down_weights, up_weights, coarse, nest_owner, nest_cell, land_weight):
    row_ids = jnp.arange(N_TX * N_TY * CELLS_C, dtype=jnp.int32)
    tile_row = row_ids // (N_TY * CELLS_C)
    coarse_rows = (tile_row * N_TY + nest_owner[:, 0]) * CELLS_C + nest_cell
    fetched = coarse[coarse_rows].reshape(N_TX, N_TY, HT // 4, WT // 4, C)
    fetched = jnp.transpose(fetched, (0, 2, 1, 3, 4)).reshape(N_TX * (HT // 4), N_TY * (WT // 4), C)
    condition = enlarge(fetched, 4).astype(jnp.float32)
    land_up = enlarge(land_weight.astype(jnp.float32), 4)[:, :, None]
    scaling = 1.0 / float(NH * NW) ** 0.5
    pad_one = ((1, 1), (1, 1), (0, 0))
    outputs, in_grads, down_list, up_list = ([], [], [], [])
    for segment_id in range(N_SEGMENT):
        decoder = 1.0 if segment_id >= N_SEGMENT // 2 else 0.0
        encoder = 1.0 - decoder
        down_kernel = down_weights[segment_id]
        up_kernel = up_weights[segment_id]
        block_in = (act_in[segment_id].astype(jnp.float32) + decoder * partner_in[segment_id].astype(jnp.float32) + condition).astype(jnp.bfloat16)
        pre_down, raised = lower_parts(block_in, down_kernel)
        output = (block_in.astype(jnp.float32) + convolve(raised, up_kernel, 1, ((1, 1), (1, 1)), 1)).astype(jnp.bfloat16)
        weighting = land_up if segment_id == N_SEGMENT - 1 else 1.0
        out_grad = ((grad_in[segment_id].astype(jnp.float32) + encoder * partner_in[segment_id].astype(jnp.float32)) * weighting).astype(jnp.bfloat16)
        pre_back, raised_back = lower_parts(stashed[segment_id], down_kernel)
        raised_grad = convolve(out_grad, flipped(up_kernel), 1, ((1, 1), (1, 1)), 1)
        pre_grad = (pooled(raised_grad) * silu_slope(pre_back)).astype(jnp.bfloat16)
        in_grad = (out_grad.astype(jnp.float32) + convolve(pre_grad, flipped(down_kernel), 1, ((1, 2), (1, 2)), 2)).astype(jnp.bfloat16)
        up_list.append(kernel_grad(jnp.pad(raised_back, pad_one), out_grad, 1) * scaling)
        down_list.append(kernel_grad(jnp.pad(stashed[segment_id], pad_one), pre_grad, 2) * scaling)
        outputs.append(output)
        in_grads.append(in_grad)
    blank = jnp.zeros_like(outputs[0])
    act_out = jnp.stack([blank] + outputs[:N_SEGMENT - 1])
    grad_out = jnp.stack(in_grads[1:] + [blank])
    partner_list = []
    for segment_id in range(N_SEGMENT):
        mirror = N_SEGMENT - 1 - segment_id
        partner_list.append(outputs[mirror] if segment_id >= N_SEGMENT // 2 else in_grads[mirror])
    partner_out = jnp.stack(partner_list)
    return (act_out, grad_out, partner_out, jnp.stack(down_list), jnp.stack(up_list))
```

```python
import functools
import math

import jax
import jax.numpy as jnp
from jax import lax
from jax.experimental import pallas as pl
from jax.experimental.pallas import tpu as pltpu
from jax.sharding import PartitionSpec as P

F32 = jnp.float32
BF = jnp.bfloat16
MESH = pl.DeviceIdType.MESH

HT, WT, C, C2 = 16, 64, 128, 192
CP = 256
H2, W2 = HT // 2, WT // 2
M2 = H2 * W2
CELLS, CAP = 64, 8
NSEG, NTX, NTY = 4, 8, 16
NY, NZ = 4, 16
ROWS = 1728
QUART = ROWS // NY
PIECE = QUART // NZ
PADP = 32
TAPS_OF = ((2,), (1, 2), (0, 1), (0,))


def dot(a, b, dims=((1,), (0,))):
    return lax.dot_general(a, b, (dims, ((), ())), preferred_element_type=F32)


def rows_of(view, index):
    lanes = view.shape[-1]
    pairs = view.reshape(view.shape[0] // 2, 2, W2, lanes)
    start = index // 2
    return pairs[start : start + H2, index % 2].reshape(M2, lanes)


def kernel(
    act, par, sta, gra, dw, uw, coarse, nown, ncell, land,
    left_out, right_out, down_out, up_out,
    dwp, uc, t32, g32, soo, see, goo, gee, dim, wim,
    prb, pgf, rpf, r32, pw, gds, gf, gs, zs, zp, fs,
    pay_ig, pay_out,
    rqs, rqr, rps, rpr, condb, tr,
    srow_s, ogup_s, colr_s, coll_s,
    top_r, bot_r, lft_r, rgt_r, ctl_r, ctr_r, cbl_r, cbr_r,
    pgrow_s, pgcol_s, pgrow_r, pgcol_r, pgcor_r,
    birow_s, bicol_s, birow_r, bicol_r, bicor_r,
    rdt_s, rdb_s, rdl_s, rdr_s,
    rdt_r, rdb_r, rdl_r, rdr_r, rtl_r, rtr_r, rbl_r, rbr_r,
    gb, ra, yb, ry, zb, rz, fin, rfin,
    ssem, rsem,
):
    seg, tx, ty = lax.axis_index("segment"), lax.axis_index("tx"), lax.axis_index("ty")
    core = lax.rem(ty, 2)
    zl = ty // 2
    zh = lax.rem(tx, 2)
    yy = tx // 2
    zz = zh * 8 + zl

    def at(dx, dy):
        return (seg, lax.rem(tx + dx + NTX, NTX), lax.rem(ty + dy + NTY, NTY))

    def ty_peer(q):
        return (seg, tx, lax.rem(ty + q, NTY))

    def y_peer(q):
        return (seg, lax.rem(yy + q, NY) * 2 + zh, ty)

    def z_peer(q):
        z = lax.rem(zz + q, NZ)
        return (seg, yy * 2 + z // 8, lax.rem(z, 8) * 2 + core)

    sibling = (seg, tx, zl * 2 + 1 - core)
    seg_next = (lax.rem(seg + 1, NSEG), tx, ty)
    seg_prev = (lax.rem(seg + NSEG - 1, NSEG), tx, ty)

    barrier = pltpu.get_barrier_semaphore()
    around = [(1, 0), (-1, 0), (0, 1), (0, -1), (1, 1), (1, -1), (-1, 1), (-1, -1)]
    greeted = [ty_peer(q) for q in range(1, NTY)]
    greeted += [at(dx, dy) for dx, dy in around if dx != 0]
    greeted += [y_peer(q) for q in range(1, NY)]
    greeted += [z_peer(q) for q in range(1, NZ)]
    greeted += [seg_next, seg_prev]
    for device in greeted:
        pl.semaphore_signal(barrier, inc=1, device_id=device, device_id_type=MESH)

    count = [0]
    started = []

    def slot():
        count[0] += 1
        return count[0] - 1

    def make(index, src, dst, device):
        return pltpu.make_async_remote_copy(
            src_ref=src, dst_ref=dst, send_sem=ssem.at[index], recv_sem=rsem.at[index],
            device_id=device, device_id_type=MESH,
        )

    def send(src, dst, device):
        copy = make(slot(), src, dst, device)
        copy.start()
        started.append(copy)
        return copy

    not_top, not_bottom = tx > 0, tx < NTX - 1
    not_left, not_right = ty > 0, ty < NTY - 1

    def keep(flag, value):
        return jnp.where(flag, value, 0.0)

    decoder = (seg >= NSEG // 2).astype(F32)
    encoder = 1.0 - decoder

    def iota(shape, axis):
        return lax.broadcasted_iota(jnp.int32, shape, axis)

    ocol = nown[...].astype(F32)
    crow = ncell[...].astype(F32)
    n0, n1 = iota((CELLS, CELLS), 0), iota((CELLS, CELLS), 1)
    orow = jnp.sum(jnp.where(n0 == n1, ocol, 0.0), axis=0, keepdims=True)
    ccol = jnp.sum(jnp.where(n0 == n1, crow, 0.0), axis=1, keepdims=True)
    same = jnp.where(ocol == orow, 1.0, 0.0)
    slot_row = jnp.sum(jnp.where(n0 < n1, same, 0.0), axis=0, keepdims=True)
    slot_col = jnp.sum(jnp.where(n1 < n0, same, 0.0), axis=1, keepdims=True)
    tyf = ty.astype(F32)

    def place(owner, slots):
        offset = owner - tyf
        return jnp.where(offset < 0.0, offset + NTY, offset) * CAP + slots

    qrow, qcol = place(orow, slot_row), place(ocol, slot_col)
    chosen = jnp.where(iota((NTY * CAP, CELLS), 0).astype(F32) == qrow, 1.0, 0.0).astype(BF)
    cell_hot = jnp.where(ccol == iota((CELLS, 128), 1).astype(F32), 1.0, 0.0).astype(BF)
    asked = dot(chosen, cell_hot)
    for q in range(NTY):
        rqs[q] = asked[q * CAP : (q + 1) * CAP].astype(BF)
    rqr[0] = rqs[0]

    spread = iota((WT, WT // 4), 1) == (iota((WT, WT // 4), 0) >> 2)
    for k in range(HT // 4):
        row = land[k : k + 1, :].astype(F32)
        weight = jnp.sum(jnp.where(spread, row, 0.0), axis=1, keepdims=True)
        weight = jnp.where(seg == NSEG - 1, weight, 1.0)
        for y in range(4 * k, 4 * k + 4):
            part = pl.ds(y * WT, WT)
            value = (gra[part, :].astype(F32) + encoder * par[part, :].astype(F32)) * weight
            g32[part, :] = value.astype(BF).astype(F32)
    t32[...] = sta[...].astype(F32)

    last = (HT - 1) * WT
    srow_s[0] = sta[last : last + WT, :]
    srow_s[1] = g32[last : last + WT, :].astype(BF)
    ogup_s[...] = g32[0:WT, :].astype(BF)
    colr_s[0] = t32[pl.ds(WT - 1, HT, stride=WT), :].astype(BF)
    colr_s[1] = g32[pl.ds(WT - 1, HT, stride=WT), :].astype(BF)
    coll_s[...] = g32[pl.ds(0, HT, stride=WT), :].astype(BF)

    pl.semaphore_wait(barrier, len(greeted))

    request = [send(rqs.at[q], rqr.at[q], ty_peer(q)) for q in range(1, NTY)]
    rim = [
        send(srow_s, top_r, at(1, 0)),
        send(ogup_s, bot_r, at(-1, 0)),
        send(colr_s, ctl_r, at(1, 1)),
        send(coll_s, ctr_r, at(1, -1)),
        send(colr_s.at[1], cbl_r, at(-1, 1)),
        send(coll_s, cbr_r, at(-1, -1)),
        send(colr_s, lft_r, at(0, 1)),
        send(coll_s, rgt_r, at(0, -1)),
    ]

    dwp[:, 0:C2] = dw[...]
    dwp[:, C2:CP] = jnp.zeros((9 * C, CP - C2), BF)
    uc[C2:CP, :] = jnp.zeros((CP - C2, 16 * C), BF)
    for u in range(4):
        for v in range(4):
            total = None
            for a in TAPS_OF[u]:
                for b in TAPS_OF[v]:
                    tap = uw[a * 3 + b].astype(F32)
                    total = tap if total is None else total + tap
            block = (u * 4 + v) * C
            uc[0:C2, block : block + C] = total.astype(BF)

    def fill(oo, ee, fine):
        ee[1:17, 0:W2, :] = fine[pl.ds(0, HT * W2, stride=2), :].reshape(HT, W2, C)
        oo[1:17, 8:40, :] = fine[pl.ds(1, HT * W2, stride=2), :].reshape(HT, W2, C)

    def fill_row(oo, ee, r, flag, row):
        tr[...] = keep(flag, row.astype(F32))
        ee[r, 0:W2, :] = tr[pl.ds(0, W2, stride=2), :]
        oo[r, 8:40, :] = tr[pl.ds(1, W2, stride=2), :]

    def fill_col(plane, first, at_col, flag, column):
        values = keep(flag, column.astype(F32))
        for r in range(values.shape[0]):
            plane[first + r, at_col : at_col + 1, :] = values[r : r + 1, :]

    def fill_cell(plane, r, at_col, flag, column, i):
        values = keep(flag, column.astype(F32))
        plane[r, at_col : at_col + 1, :] = values[i : i + 1, :]

    def put_half(value):
        r32[0] = value[:, 0:C]
        r32[1] = value[:, C:CP]

    def half_col(j):
        halves = [r32[h, pl.ds(j, H2, stride=W2), :] for h in range(2)]
        return jnp.concatenate(halves, axis=1).astype(BF)

    def gather_down(oo, ee):
        views = [oo[:, 7:39, :], ee[:, 0:32, :], oo[:, 8:40, :]]
        for b, view in enumerate(views):
            view = view.astype(BF)
            for a in range(3):
                block = (a * 3 + b) * C
                dim[:, block : block + C] = rows_of(view, a)

    fill(soo, see, t32)
    fill(goo, gee, g32)

    for copy in request:
        copy.wait_recv()
    wanted = jnp.concatenate([rqr[q].astype(F32) for q in range(NTY)], axis=0)
    answer = dot(wanted[:, 0:CELLS].astype(BF), coarse[...])
    for q in range(NTY):
        rps[q] = answer[q * CAP : (q + 1) * CAP].astype(BF)
    rpr[0] = rps[0]
    reply = [
        send(rps.at[q], rpr.at[q], (seg, tx, lax.rem(ty + NTY - q, NTY))) for q in range(1, NTY)
    ]

    for copy in rim:
        copy.wait_recv()
    fill_row(soo, see, 0, not_top, top_r[0])
    fill_row(goo, gee, 0, not_top, top_r[1])
    fill_row(goo, gee, 17, not_bottom, bot_r[...])
    fill_col(soo, 1, 7, not_left, lft_r[0])
    fill_col(goo, 1, 7, not_left, lft_r[1])
    fill_col(gee, 1, W2, not_right, rgt_r[...])
    fill_cell(soo, 0, 7, not_top & not_left, ctl_r[0], HT - 1)
    fill_cell(goo, 0, 7, not_top & not_left, ctl_r[1], HT - 1)
    fill_cell(gee, 0, W2, not_top & not_right, ctr_r[...], HT - 1)
    fill_cell(goo, 17, 7, not_bottom & not_left, cbl_r[...], 0)
    fill_cell(gee, 17, W2, not_bottom & not_right, cbr_r[...], 0)

    gather_down(soo, see)
    for v, view in enumerate([goo[:, 7:39, :], gee[:, 0:32, :], goo[:, 8:40, :], gee[:, 1:33, :]]):
        view = view.astype(BF)
        for u in range(4):
            block = (u * 4 + v) * C
            wim[:, block : block + C] = rows_of(view, u)

    pre_back = dot(dim[...], dwp[...])
    gate = jax.nn.sigmoid(pre_back)
    prb[...] = (pre_back * gate).astype(BF)
    pooled = dot(wim[...], uc[...], ((1,), (1,)))
    pre_grad = (pooled * (gate * (1.0 + pre_back * (1.0 - gate)))).astype(BF)
    half_grid = pre_grad.astype(F32)
    put_half(half_grid)
    pgrow_s[...] = half_grid[0:W2].astype(BF)
    pgcol_s[...] = half_col(0)
    pg_rim = [
        send(pgrow_s, pgrow_r, at(-1, 0)),
        send(pgcol_s, pgcor_r, at(-1, -1)),
        send(pgcol_s, pgcol_r, at(0, -1)),
    ]
    pgf[0:H2, 0:W2, :] = half_grid.reshape(H2, W2, CP)

    for copy in reply:
        copy.wait_recv()
    table = jnp.concatenate([rpr[q].astype(F32) for q in range(NTY)], axis=0).astype(BF)
    pick = jnp.where(iota((CELLS, NTY * CAP), 1).astype(F32) == qcol, 1.0, 0.0).astype(BF)
    fetched = dot(pick, table).astype(BF)
    r0, r1 = iota((4 * WT, CELLS), 0), iota((4 * WT, CELLS), 1)
    widen = jnp.where(r1 == ((r0 >> 6) << 4) + ((r0 & 63) >> 2), 1.0, 0.0).astype(BF)
    condb[...] = dot(widen, fetched)
    for y in range(HT):
        part = pl.ds(y * WT, WT)
        value = (
            act[part, :].astype(F32)
            + decoder * par[part, :].astype(F32)
            + condb[pl.ds(y // 4 * WT, WT), :]
        )
        t32[part, :] = value.astype(BF).astype(F32)
    birow_s[...] = t32[last : last + WT, :].astype(BF)
    bicol_s[...] = t32[pl.ds(WT - 1, HT, stride=WT), :].astype(BF)
    bi_rim = [
        send(birow_s, birow_r, at(1, 0)),
        send(bicol_s, bicor_r, at(1, 1)),
        send(bicol_s, bicol_r, at(0, 1)),
    ]
    fill(soo, see, t32)

    product = dot(dim[...], pre_grad, ((0,), (0,)))
    gds[0] = product[:, 0:C]
    gds[1] = product[:, C:CP]
    pw[...] = dot(prb[...], wim[...], ((0,), (0,)))
    low = iota((ROWS // 3, C), 1) < 64
    even_lo = gds[0, pl.ds(0, ROWS // 3, stride=2), :]
    even_hi = gds[1, pl.ds(0, ROWS // 3, stride=2), :]
    odd_lo = pltpu.roll(gds[0, pl.ds(1, ROWS // 3, stride=2), :], 64, 1)
    odd_hi = pltpu.roll(gds[1, pl.ds(1, ROWS // 3, stride=2), :], 64, 1)
    gf[0, pl.ds(0, ROWS // 3, stride=3), :] = even_lo
    gf[0, pl.ds(1, ROWS // 3, stride=3), :] = jnp.where(low, even_hi, odd_lo)
    gf[0, pl.ds(2, ROWS // 3, stride=3), :] = jnp.where(low, odd_lo, odd_hi)
    for a in range(3):
        for b in range(3):
            total = None
            for u in (2 - a, 3 - a):
                for v in (2 - b, 3 - b):
                    block = (u * 4 + v) * C
                    term = pw[0:C2, block : block + C]
                    total = term if total is None else total + term
            tap = (a * 3 + b) * C2
            gf[1, tap : tap + C2, :] = total
    gb[...] = gf[1 - core].astype(BF)
    swap = send(gb, ra, sibling)

    for copy in pg_rim:
        copy.wait_recv()
    pgf[H2, 0:W2, :] = keep(not_bottom, pgrow_r[...].astype(F32))
    fill_col(pgf, 0, W2, not_right, pgcol_r[...])
    fill_cell(pgf, H2, W2, not_bottom & not_right, pgcor_r[...], 0)
    shifted = [
        [pgf[di : di + H2, dj : dj + W2, :].astype(BF).reshape(M2, CP) for dj in (0, 1)]
        for di in (0, 1)
    ]

    def spread_out(value, pr, pc):
        for i in range(H2):
            t32[pl.ds((2 * i + pr) * WT + pc, W2, stride=2), :] = value[i * W2 : (i + 1) * W2]

    for pr in range(2):
        for pc in range(2):
            plane = gee[:, 0:32, :] if pc == 0 else goo[:, 8:40, :]
            value = rows_of(plane, 1 + pr)
            for a, di in ((1, 0),) if pr == 0 else ((2, 0), (0, 1)):
                for b, dj in ((1, 0),) if pc == 0 else ((2, 0), (0, 1)):
                    tap = (a * 3 + b) * C
                    value = value + dot(shifted[di][dj], dwp[tap : tap + C, :], ((1,), (1,)))
            spread_out(value, pr, pc)
    pay_ig[...] = t32[...].astype(BF)

    up_slot, down_slot = slot(), slot()
    ig_next = make(up_slot, pay_ig, left_out, seg_next)
    ig_prev = make(down_slot, pay_ig, right_out, seg_prev)
    out_next = make(up_slot, pay_out, left_out, seg_next)
    out_prev = make(down_slot, pay_out, right_out, seg_prev)

    @pl.when(seg == NSEG - 1)
    def _():
        ig_next.start()

    @pl.when(seg >= 1)
    def _():
        ig_prev.start()

    for copy in bi_rim:
        copy.wait_recv()
    fill_row(soo, see, 0, not_top, birow_r[...])
    fill_col(soo, 1, 7, not_left, bicol_r[...])
    fill_cell(soo, 0, 7, not_top & not_left, bicor_r[...], HT - 1)
    gather_down(soo, see)
    pre_down = dot(dim[...], dwp[...])
    half_grid = (pre_down * jax.nn.sigmoid(pre_down)).astype(BF).astype(F32)
    put_half(half_grid)
    rdt_s[...] = half_grid[0:W2].astype(BF)
    rdb_s[...] = half_grid[M2 - W2 : M2].astype(BF)
    rdl_s[...] = half_col(0)
    rdr_s[...] = half_col(W2 - 1)
    red_rim = [
        send(rdb_s, rdt_r, at(1, 0)),
        send(rdt_s, rdb_r, at(-1, 0)),
        send(rdr_s, rtl_r, at(1, 1)),
        send(rdl_s, rtr_r, at(1, -1)),
        send(rdr_s, rbl_r, at(-1, 1)),
        send(rdl_s, rbr_r, at(-1, -1)),
        send(rdr_s, rdl_r, at(0, 1)),
        send(rdl_s, rdr_r, at(0, -1)),
    ]
    rpf[1 : H2 + 1, 8:40, :] = half_grid.reshape(H2, W2, CP)

    swap.wait_recv()
    gs[...] = gf[core] + ra[...].astype(F32)
    yb[...] = gs[...].astype(BF).reshape(NY, QUART, C)
    y_sum = [send(yb.at[lax.rem(yy + q, NY)], ry.at[q - 1], y_peer(q)) for q in range(1, NY)]

    for copy in red_rim:
        copy.wait_recv()
    rpf[0, 8:40, :] = keep(not_top, rdt_r[...].astype(F32))
    rpf[H2 + 1, 8:40, :] = keep(not_bottom, rdb_r[...].astype(F32))
    fill_col(rpf, 1, 7, not_left, rdl_r[...])
    fill_col(rpf, 1, 40, not_right, rdr_r[...])
    fill_cell(rpf, 0, 7, not_top & not_left, rtl_r[...], H2 - 1)
    fill_cell(rpf, 0, 40, not_top & not_right, rtr_r[...], H2 - 1)
    fill_cell(rpf, H2 + 1, 7, not_bottom & not_left, rbl_r[...], 0)
    fill_cell(rpf, H2 + 1, 40, not_bottom & not_right, rbr_r[...], 0)
    moved = {}
    for dj in range(3):
        view = rpf[:, 7 + dj : 39 + dj, :].astype(BF)
        for di in range(3):
            moved[di, dj] = view[di : di + H2].reshape(M2, CP)
    meets = (((0, 3), (1, 1)), ((1, 2), (2, 0)))
    for pr in range(2):
        for pc in range(2):
            plane = see[:, 0:32, :] if pc == 0 else soo[:, 8:40, :]
            value = rows_of(plane, 1 + pr)
            for di, u in meets[pr]:
                for dj, v in meets[pc]:
                    block = (u * 4 + v) * C
                    value = value + dot(moved[di, dj], uc[:, block : block + C])
            spread_out(value, pr, pc)
    pay_out[...] = t32[...].astype(BF)

    @pl.when(seg <= NSEG - 2)
    def _():
        out_next.start()

    @pl.when(seg == 0)
    def _():
        out_prev.start()

    for copy in y_sum:
        copy.wait_recv()
    total = gs[pl.ds(yy * QUART, QUART), :]
    for q in range(NY - 1):
        total = total + ry[q].astype(F32)
    zs[0:QUART, :] = total
    zs[QUART:, :] = jnp.zeros((zs.shape[0] - QUART, C), F32)
    for z in range(NZ):
        zp[z] = zs[z * PIECE : z * PIECE + PADP, :]
    zb[...] = zp[...].astype(BF)
    z_sum = [send(zb.at[lax.rem(zz + q, NZ)], rz.at[q - 1], z_peer(q)) for q in range(1, NZ)]
    for copy in z_sum:
        copy.wait_recv()
    total = zp[zz]
    for q in range(NZ - 1):
        total = total + rz[q].astype(F32)
    scaling = 1.0 / math.sqrt(HT * WT * NTX * NTY)
    fin[...] = total * scaling
    last_swap = send(fin, rfin, sibling)
    last_swap.wait_recv()
    mine, other = fin[...], rfin[...]
    first = core == 0
    head = iota((16, C), 1) < 64
    for out, value in ((down_out, jnp.where(first, mine, other)), (up_out, jnp.where(first, other, mine))):
        fs[...] = pltpu.roll(value, 64, 1)
        second_half = jnp.where(head, fs[13:29, :], fs[14:30, :])
        half = jnp.where(first, value[0:16], second_half)
        for r in range(13):
            out[0:1, r * C : (r + 1) * C] = half[r : r + 1, :]
        out[0:1, 13 * C : 13 * C + 64] = half[13:14, 0:64]

    out_next.wait_recv()
    out_prev.wait_recv()
    out_next.wait_send()
    out_prev.wait_send()
    for copy in started:
        copy.wait_send()


N_COPIES = 15 + 8 + 15 + 3 + 3 + 1 + 2 + 8 + 3 + 15 + 1


def whole_step(act, par, sta, gra, dw, uw, coarse, nown, ncell, land):
    vm = pltpu.VMEM
    fine_rows = HT * WT
    scratch = [
        vm((9 * C, CP), BF), vm((CP, 16 * C), BF), vm((fine_rows, C), F32), vm((fine_rows, C), F32),
        vm((18, 40, C), F32), vm((18, 40, C), F32), vm((18, 40, C), F32), vm((18, 40, C), F32),
        vm((M2, 9 * C), BF), vm((M2, 16 * C), BF),
        vm((M2, CP), BF), vm((H2 + 1, 40, CP), F32), vm((H2 + 2, 48, CP), F32), vm((2, M2, C), F32),
        vm((CP, 16 * C), F32), vm((2, 9 * C, C), F32), vm((2, ROWS, C), F32), vm((ROWS, C), F32),
        vm((448, C), F32), vm((NZ, PADP, C), F32), vm((PADP, C), F32),
        vm((fine_rows, C), BF), vm((fine_rows, C), BF),
        vm((NTY, CAP, 128), BF), vm((NTY, CAP, 128), BF), vm((NTY, CAP, C), BF), vm((NTY, CAP, C), BF),
        vm((4 * WT, C), F32), vm((WT, C), F32),
        vm((2, WT, C), BF), vm((WT, C), BF), vm((2, HT, C), BF), vm((HT, C), BF),
        vm((2, WT, C), BF), vm((WT, C), BF), vm((2, HT, C), BF), vm((HT, C), BF),
        vm((2, HT, C), BF), vm((HT, C), BF), vm((HT, C), BF), vm((HT, C), BF),
        vm((W2, CP), BF), vm((H2, CP), BF), vm((W2, CP), BF), vm((H2, CP), BF), vm((H2, CP), BF),
        vm((WT, C), BF), vm((HT, C), BF), vm((WT, C), BF), vm((HT, C), BF), vm((HT, C), BF),
        vm((W2, CP), BF), vm((W2, CP), BF), vm((H2, CP), BF), vm((H2, CP), BF),
        vm((W2, CP), BF), vm((W2, CP), BF), vm((H2, CP), BF), vm((H2, CP), BF),
        vm((H2, CP), BF), vm((H2, CP), BF), vm((H2, CP), BF), vm((H2, CP), BF),
        vm((ROWS, C), BF), vm((ROWS, C), BF), vm((NY, QUART, C), BF), vm((NY - 1, QUART, C), BF),
        vm((NZ, PADP, C), BF), vm((NZ - 1, PADP, C), BF), vm((PADP, C), F32), vm((PADP, C), F32),
        pltpu.SemaphoreType.DMA((N_COPIES,)), pltpu.SemaphoreType.DMA((N_COPIES,)),
    ]
    in_vmem = pl.BlockSpec(memory_space=pltpu.VMEM)
    return pl.pallas_call(
        kernel,
        out_shape=(
            jax.ShapeDtypeStruct((fine_rows, C), BF),
            jax.ShapeDtypeStruct((fine_rows, C), BF),
            jax.ShapeDtypeStruct((1, ROWS), F32),
            jax.ShapeDtypeStruct((1, ROWS), F32),
        ),
        in_specs=[in_vmem] * 10,
        out_specs=(
            pl.BlockSpec(memory_space=pl.ANY), pl.BlockSpec(memory_space=pl.ANY), in_vmem, in_vmem,
        ),
        scratch_shapes=scratch,
        compiler_params=pltpu.CompilerParams(
            collective_id=0, has_side_effects=True, vmem_limit_bytes=56 << 20
        ),
        name="relay",
    )(act, par, sta, gra, dw, uw, coarse, nown, ncell, land)


def local(
    act_in, partner_in, stashed, grad_in, down_weights, up_weights, coarse, nest_owner, nest_cell,
    land_weight,
):
    flat = (HT * WT, C)
    from_before, from_after, down_sum, up_sum = whole_step(
        act_in.reshape(flat), partner_in.reshape(flat), stashed.reshape(flat), grad_in.reshape(flat),
        down_weights.reshape(9 * C, C2), up_weights.reshape(9, C2, C), coarse, nest_owner,
        nest_cell.reshape(1, CELLS), land_weight,
    )
    position = lax.axis_index("segment")
    zero = jnp.zeros((), BF)
    act_out = jnp.where(position == 0, zero, from_before)
    grad_out = jnp.where(position == NSEG - 1, zero, from_after)
    partner_out = jnp.where(position % 2 == 0, from_before, from_after)
    tile = (1, HT, WT, C)
    return (
        act_out.reshape(tile), grad_out.reshape(tile), partner_out.reshape(tile), down_sum, up_sum,
    )


def solution(mesh):
    placed = (
        P("segment", "tx", "ty", None),
        P("segment", "tx", "ty", None),
        P("segment", "tx", "ty", None),
        P("segment", "tx", "ty", None),
        P("segment", None, None, None, None),
        P("segment", None, None, None, None),
        P(("tx", "ty"), None),
        P(("tx", "ty"), None),
        P(("tx", "ty")),
        P("tx", "ty"),
    )
    return jax.shard_map(
        local,
        mesh=mesh,
        in_specs=placed,
        out_specs=(
            P("segment", "tx", "ty", None),
            P("segment", "tx", "ty", None),
            P("segment", "tx", "ty", None),
            P("segment", ("tx", "ty")),
            P("segment", ("tx", "ty")),
        ),
        check_vma=False,
    )
```

```python
import functools
import math

import jax
import jax.numpy as jnp
from jax import lax
from jax.experimental import pallas as pl
from jax.experimental.pallas import tpu as pltpu
from jax.sharding import PartitionSpec as P

F32 = jnp.float32
BF = jnp.bfloat16
MESH = pl.DeviceIdType.MESH

HT, WT, C, C2 = 16, 64, 128, 192
CP = 256
H2, W2 = HT // 2, WT // 2
M2 = H2 * W2
CELLS, CAP = 64, 8
NSEG, NTX, NTY = 4, 8, 16
NY, NZ = 4, 16
ROWS = 1728
QUART = ROWS // NY
PIECE = QUART // NZ
PADP = 32
TAPS_OF = ((2,), (1, 2), (0, 1), (0,))


def dot(a, b, dims=((1,), (0,))):
    return lax.dot_general(a, b, (dims, ((), ())), preferred_element_type=F32)


def rows_of(view, index):
    lanes = view.shape[-1]
    pairs = view.reshape(view.shape[0] // 2, 2, W2, lanes)
    start = index // 2
    return pairs[start : start + H2, index % 2].reshape(M2, lanes)


def kernel(
    act_h, par_h, sta_h, gra_h, dw_h, uw_h, coarse_h, nown_h, ncell_h, land_h,
    left_out, right_out, down_out, up_out,
    act, par, sta, gra, dw, uw, coarse, nown, ncell, land,
    dwp, uc, t32, g32, b32, soo, see, goo, gee, boo, bee, dim, dimf, dimg, wim,
    prb, pgf, rpf, r32, pw, gds, gf, gs, zs, zp, fs,
    pay_ig, pay_out,
    rqs, rqr, rps, rpr, condb, tr,
    srow_s, ogup_s, colr_s, coll_s,
    top_r, bot_r, lft_r, rgt_r, ctl_r, ctr_r, cbl_r, cbr_r,
    pgrow_s, pgcol_s, pgrow_r, pgcol_r, pgcor_r,
    birow_s, biup_s, bicol_s, birow_r, biup_r, bicol_r, bicor_r, bibl_r,
    rdb_s, rdl_s, rdr_s, rel_s, rer_s,
    rdt_r, rdl_r, rdr_r, rtl_r, rtr_r, rel_r, rer_r,
    gb, ra, yb, ry, zb, rz, fin, rfin,
    ssem, rsem, isem,
):
    bring = [
        pltpu.make_async_copy(src, dst, isem.at[i])
        for i, (src, dst) in enumerate((
            (nown_h, nown), (ncell_h, ncell), (land_h, land), (gra_h, gra), (par_h, par), (sta_h, sta),
            (coarse_h, coarse), (act_h, act), (uw_h, uw), (dw_h, dw),
        ))
    ]
    for copy in bring:
        copy.start()

    seg, tx, ty = lax.axis_index("segment"), lax.axis_index("tx"), lax.axis_index("ty")
    core = lax.rem(ty, 2)
    zl = ty // 2
    zh = lax.rem(tx, 2)
    yy = tx // 2
    zz = zh * 8 + zl

    def at(dx, dy):
        return (seg, lax.rem(tx + dx + NTX, NTX), lax.rem(ty + dy + NTY, NTY))

    def ty_peer(q):
        return (seg, tx, lax.rem(ty + q, NTY))

    def y_peer(q):
        return (seg, lax.rem(yy + q, NY) * 2 + zh, ty)

    def z_peer(q):
        z = lax.rem(zz + q, NZ)
        return (seg, yy * 2 + z // 8, lax.rem(z, 8) * 2 + core)

    sibling = (seg, tx, zl * 2 + 1 - core)
    seg_next = (lax.rem(seg + 1, NSEG), tx, ty)
    seg_prev = (lax.rem(seg + NSEG - 1, NSEG), tx, ty)

    barrier = pltpu.get_barrier_semaphore()
    around = [(1, 0), (-1, 0), (0, 1), (0, -1), (1, 1), (1, -1), (-1, 1), (-1, -1)]
    greeted = [ty_peer(q) for q in range(1, NTY)]
    greeted += [at(dx, dy) for dx, dy in around if dx != 0]
    greeted += [y_peer(q) for q in range(1, NY)]
    greeted += [z_peer(q) for q in range(1, NZ)]
    greeted += [seg_next, seg_prev]
    for device in greeted:
        pl.semaphore_signal(barrier, inc=1, device_id=device, device_id_type=MESH)

    count = [0]
    started = []

    def slot():
        count[0] += 1
        return count[0] - 1

    def make(index, src, dst, device):
        return pltpu.make_async_remote_copy(
            src_ref=src, dst_ref=dst, send_sem=ssem.at[index], recv_sem=rsem.at[index],
            device_id=device, device_id_type=MESH,
        )

    def send(src, dst, device):
        copy = make(slot(), src, dst, device)
        copy.start()
        started.append(copy)
        return copy

    def arrived(name, copies):
        with jax.named_scope("await_" + name):
            for copy in copies:
                copy.wait_recv()

    not_top, not_bottom = tx > 0, tx < NTX - 1
    not_left, not_right = ty > 0, ty < NTY - 1

    def keep(flag, value):
        return jnp.where(flag, value, 0.0)

    for copy in bring[:3]:
        copy.wait()
    decoder = (seg >= NSEG // 2).astype(F32)
    encoder = 1.0 - decoder

    def iota(shape, axis):
        return lax.broadcasted_iota(jnp.int32, shape, axis)

    orow = nown[...].astype(F32)
    crow = ncell[...].astype(F32)
    n0, n1 = iota((CELLS, CELLS), 0), iota((CELLS, CELLS), 1)
    ocol = jnp.sum(jnp.where(n0 == n1, orow, 0.0), axis=1, keepdims=True)
    ccol = jnp.sum(jnp.where(n0 == n1, crow, 0.0), axis=1, keepdims=True)
    same = jnp.where(ocol == orow, 1.0, 0.0)
    slot_row = jnp.sum(jnp.where(n0 < n1, same, 0.0), axis=0, keepdims=True)
    slot_col = jnp.sum(jnp.where(n1 < n0, same, 0.0), axis=1, keepdims=True)
    tyf = ty.astype(F32)

    def place(owner, slots):
        offset = owner - tyf
        return jnp.where(offset < 0.0, offset + NTY, offset) * CAP + slots

    qrow, qcol = place(orow, slot_row), place(ocol, slot_col)
    chosen = jnp.where(iota((NTY * CAP, CELLS), 0).astype(F32) == qrow, 1.0, 0.0).astype(BF)
    cell_hot = jnp.where(ccol == iota((CELLS, 128), 1).astype(F32), 1.0, 0.0).astype(BF)
    asked = dot(chosen, cell_hot)
    for q in range(NTY):
        rqs[q] = asked[q * CAP : (q + 1) * CAP].astype(BF)
    rqr[0] = rqs[0]

    for copy in bring[3:6]:
        copy.wait()
    spread = iota((WT, WT // 4), 1) == (iota((WT, WT // 4), 0) >> 2)
    for k in range(HT // 4):
        row = land[k : k + 1, :].astype(F32)
        weight = jnp.sum(jnp.where(spread, row, 0.0), axis=1, keepdims=True)
        weight = jnp.where(seg == NSEG - 1, weight, 1.0)
        for y in range(4 * k, 4 * k + 4):
            part = pl.ds(y * WT, WT)
            value = (gra[part, :].astype(F32) + encoder * par[part, :].astype(F32)) * weight
            g32[part, :] = value.astype(BF).astype(F32)
    t32[...] = sta[...].astype(F32)

    last = (HT - 1) * WT
    srow_s[0] = sta[last : last + WT, :]
    srow_s[1] = g32[last : last + WT, :].astype(BF)
    ogup_s[...] = g32[0:WT, :].astype(BF)
    colr_s[0] = t32[pl.ds(WT - 1, HT, stride=WT), :].astype(BF)
    colr_s[1] = g32[pl.ds(WT - 1, HT, stride=WT), :].astype(BF)
    coll_s[...] = g32[pl.ds(0, HT, stride=WT), :].astype(BF)

    with jax.named_scope("await_entry"):
        pl.semaphore_wait(barrier, len(greeted))

    request = [send(rqs.at[q], rqr.at[q], ty_peer(q)) for q in range(1, NTY)]
    rim = [
        send(srow_s, top_r, at(1, 0)),
        send(ogup_s, bot_r, at(-1, 0)),
        send(colr_s, ctl_r, at(1, 1)),
        send(coll_s, ctr_r, at(1, -1)),
        send(colr_s.at[1], cbl_r, at(-1, 1)),
        send(coll_s, cbr_r, at(-1, -1)),
        send(colr_s, lft_r, at(0, 1)),
        send(coll_s, rgt_r, at(0, -1)),
    ]

    for copy in bring[6:]:
        copy.wait()
    dwp[C2:CP, :] = jnp.zeros((CP - C2, 9 * C), BF)
    for t in range(9):
        dwp[0:C2, t * C : (t + 1) * C] = dw[t]
    uc[C2:CP, :] = jnp.zeros((CP - C2, 16 * C), BF)
    for u in range(4):
        for v in range(4):
            total = None
            for a in TAPS_OF[u]:
                for b in TAPS_OF[v]:
                    tap = uw[a * 3 + b].astype(F32)
                    total = tap if total is None else total + tap
            block = (u * 4 + v) * C
            uc[0:C2, block : block + C] = total.astype(BF)

    def fill(oo, ee, fine):
        ee[1:17, 0:W2, :] = fine[pl.ds(0, HT * W2, stride=2), :].reshape(HT, W2, C)
        oo[1:17, 8:40, :] = fine[pl.ds(1, HT * W2, stride=2), :].reshape(HT, W2, C)

    def fill_row(oo, ee, r, flag, row):
        tr[...] = keep(flag, row.astype(F32))
        ee[r, 0:W2, :] = tr[pl.ds(0, W2, stride=2), :]
        oo[r, 8:40, :] = tr[pl.ds(1, W2, stride=2), :]

    def fill_col(plane, first, at_col, flag, column):
        values = keep(flag, column.astype(F32))
        for r in range(values.shape[0]):
            plane[first + r, at_col : at_col + 1, :] = values[r : r + 1, :]

    def fill_cell(plane, r, at_col, flag, column, i):
        values = keep(flag, column.astype(F32))
        plane[r, at_col : at_col + 1, :] = values[i : i + 1, :]

    def put_half(value):
        r32[0] = value[:, 0:C]
        r32[1] = value[:, C:CP]

    def half_col(j):
        halves = [r32[h, pl.ds(j, H2, stride=W2), :] for h in range(2)]
        return jnp.concatenate(halves, axis=1).astype(BF)

    def gather_down(oo, ee, first, n, lhs, row):
        span = slice(2 * first, 2 * first + 2 * n + 2)
        for b, view in enumerate([oo[span, 7:39, :], ee[span, 0:32, :], oo[span, 8:40, :]]):
            pairs = view.astype(BF).reshape(n + 1, 2, W2, C)
            for a in range(3):
                block = (a * 3 + b) * C
                part = pairs[a // 2 : a // 2 + n, a % 2].reshape(n * W2, C)
                lhs[row : row + n * W2, block : block + C] = part

    fill(soo, see, t32)
    fill(goo, gee, g32)

    arrived("request", request)
    wanted = jnp.concatenate([rqr[q].astype(F32) for q in range(NTY)], axis=0)
    answer = dot(wanted[:, 0:CELLS].astype(BF), coarse[...])
    for q in range(NTY):
        rps[q] = answer[q * CAP : (q + 1) * CAP].astype(BF)
    rpr[0] = rps[0]
    reply = [
        send(rps.at[q], rpr.at[q], (seg, tx, lax.rem(ty + NTY - q, NTY))) for q in range(1, NTY)
    ]

    arrived("rim", rim)
    fill_row(soo, see, 0, not_top, top_r[0])
    fill_row(goo, gee, 0, not_top, top_r[1])
    fill_row(goo, gee, 17, not_bottom, bot_r[...])
    fill_col(soo, 1, 7, not_left, lft_r[0])
    fill_col(goo, 1, 7, not_left, lft_r[1])
    fill_col(gee, 1, W2, not_right, rgt_r[...])
    fill_cell(soo, 0, 7, not_top & not_left, ctl_r[0], HT - 1)
    fill_cell(goo, 0, 7, not_top & not_left, ctl_r[1], HT - 1)
    fill_cell(gee, 0, W2, not_top & not_right, ctr_r[...], HT - 1)
    fill_cell(goo, 17, 7, not_bottom & not_left, cbl_r[...], 0)
    fill_cell(gee, 17, W2, not_bottom & not_right, cbr_r[...], 0)

    gather_down(soo, see, 0, H2, dim, 0)
    for v, view in enumerate([goo[:, 7:39, :], gee[:, 0:32, :], goo[:, 8:40, :], gee[:, 1:33, :]]):
        view = view.astype(BF)
        for u in range(4):
            block = (u * 4 + v) * C
            wim[:, block : block + C] = rows_of(view, u)

    pre_back = dot(dim[...], dwp[...], ((1,), (1,)))
    gate = jax.nn.sigmoid(pre_back)
    prb[...] = (pre_back * gate).astype(BF)
    pooled = dot(wim[...], uc[...], ((1,), (1,)))
    pre_grad = (pooled * (gate * (1.0 + pre_back * (1.0 - gate)))).astype(BF)
    half_grid = pre_grad.astype(F32)
    put_half(half_grid)
    pgrow_s[...] = half_grid[0:W2].astype(BF)
    pgcol_s[...] = half_col(0)
    pg_rim = [
        send(pgrow_s, pgrow_r, at(-1, 0)),
        send(pgcol_s, pgcor_r, at(-1, -1)),
        send(pgcol_s, pgcol_r, at(0, -1)),
    ]
    pgf[0:H2, 0:W2, :] = half_grid.reshape(H2, W2, CP)

    product = dot(dim[...], pre_grad, ((0,), (0,)))
    gds[0] = product[:, 0:C]
    gds[1] = product[:, C:CP]
    pw[...] = dot(prb[...], wim[...], ((0,), (0,)))
    low = iota((ROWS // 3, C), 1) < 64
    even_lo = gds[0, pl.ds(0, ROWS // 3, stride=2), :]
    even_hi = gds[1, pl.ds(0, ROWS // 3, stride=2), :]
    odd_lo = pltpu.roll(gds[0, pl.ds(1, ROWS // 3, stride=2), :], 64, 1)
    odd_hi = pltpu.roll(gds[1, pl.ds(1, ROWS // 3, stride=2), :], 64, 1)
    gf[0, pl.ds(0, ROWS // 3, stride=3), :] = even_lo
    gf[0, pl.ds(1, ROWS // 3, stride=3), :] = jnp.where(low, even_hi, odd_lo)
    gf[0, pl.ds(2, ROWS // 3, stride=3), :] = jnp.where(low, odd_lo, odd_hi)
    for a in range(3):
        for b in range(3):
            total = None
            for u in (2 - a, 3 - a):
                for v in (2 - b, 3 - b):
                    block = (u * 4 + v) * C
                    term = pw[0:C2, block : block + C]
                    total = term if total is None else total + term
            tap = (a * 3 + b) * C2
            gf[1, tap : tap + C2, :] = total
    gb[...] = gf[1 - core].astype(BF)
    swap = send(gb, ra, sibling)

    arrived("swap", [swap])
    gs[...] = gf[core] + ra[...].astype(F32)
    yb[...] = gs[...].astype(BF).reshape(NY, QUART, C)
    y_sum = [send(yb.at[lax.rem(yy + q, NY)], ry.at[q - 1], y_peer(q)) for q in range(1, NY)]

    arrived("reply", reply)
    table = jnp.concatenate([rpr[q].astype(F32) for q in range(NTY)], axis=0).astype(BF)
    pick = jnp.where(iota((CELLS, NTY * CAP), 1).astype(F32) == qcol, 1.0, 0.0).astype(BF)
    fetched = dot(pick, table).astype(BF)
    r0, r1 = iota((4 * WT, CELLS), 0), iota((4 * WT, CELLS), 1)
    widen = jnp.where(r1 == ((r0 >> 6) << 4) + ((r0 & 63) >> 2), 1.0, 0.0).astype(BF)
    condb[...] = dot(widen, fetched)
    for y in range(HT):
        part = pl.ds(y * WT, WT)
        value = (
            act[part, :].astype(F32)
            + decoder * par[part, :].astype(F32)
            + condb[pl.ds(y // 4 * WT, WT), :]
        )
        b32[part, :] = value.astype(BF).astype(F32)
    birow_s[...] = b32[last : last + WT, :].astype(BF)
    bicol_s[...] = b32[pl.ds(WT - 1, HT, stride=WT), :].astype(BF)
    biup_s[...] = b32[0 : 2 * WT, :].astype(BF)
    bi_tx = [
        send(birow_s, birow_r, at(1, 0)),
        send(biup_s, biup_r, at(-1, 0)),
        send(bicol_s, bicor_r, at(1, 1)),
        send(bicol_s, bibl_r, at(-1, 1)),
    ]
    bi_ty = [send(bicol_s, bicol_r, at(0, 1))]
    fill(boo, bee, b32)

    arrived("pg_rim", pg_rim)
    pgf[H2, 0:W2, :] = keep(not_bottom, pgrow_r[...].astype(F32))
    fill_col(pgf, 0, W2, not_right, pgcol_r[...])
    fill_cell(pgf, H2, W2, not_bottom & not_right, pgcor_r[...], 0)
    shifted = [
        [pgf[di : di + H2, dj : dj + W2, :].astype(BF).reshape(M2, CP) for dj in (0, 1)]
        for di in (0, 1)
    ]

    def spread_out(value, pr, pc):
        for i in range(H2):
            t32[pl.ds((2 * i + pr) * WT + pc, W2, stride=2), :] = value[i * W2 : (i + 1) * W2]

    for pr in range(2):
        for pc in range(2):
            plane = gee[:, 0:32, :] if pc == 0 else goo[:, 8:40, :]
            value = rows_of(plane, 1 + pr)
            for a, di in ((1, 0),) if pr == 0 else ((2, 0), (0, 1)):
                for b, dj in ((1, 0),) if pc == 0 else ((2, 0), (0, 1)):
                    tap = (a * 3 + b) * C
                    value = value + dot(shifted[di][dj], dwp[:, tap : tap + C])
            spread_out(value, pr, pc)
    pay_ig[...] = t32[...].astype(BF)

    parts = [pl.ds(3 * WT, 12 * WT), pl.ds(0, 3 * WT), pl.ds(15 * WT, WT)]
    slots = [(slot(), slot()) for _ in parts]

    def block_copies(source):
        return [
            (make(up, source.at[part, :], left_out.at[part, :], seg_next),
             make(down, source.at[part, :], right_out.at[part, :], seg_prev))
            for part, (up, down) in zip(parts, slots)
        ]

    ig_copies, out_copies = block_copies(pay_ig), block_copies(pay_out)

    @pl.when(seg == NSEG - 1)
    def _():
        for copy, _ in ig_copies:
            copy.start()

    @pl.when(seg >= 1)
    def _():
        for _, copy in ig_copies:
            copy.start()

    def send_output(which):
        @pl.when(seg <= NSEG - 2)
        def _():
            for k in which:
                out_copies[k][0].start()

        @pl.when(seg == 0)
        def _():
            for k in which:
                out_copies[k][1].start()

    def reduce(lhs):
        pre_down = dot(lhs[...], dwp[...], ((1,), (1,)))
        return (pre_down * jax.nn.sigmoid(pre_down)).astype(BF).astype(F32)

    arrived("bi_ty", bi_ty)
    fill_col(boo, 1, 7, not_left, bicol_r[...])
    gather_down(boo, bee, 1, H2 - 1, dimf, 0)
    half_grid = reduce(dimf)
    r32[0, W2:M2, :] = half_grid[:, 0:C]
    r32[1, W2:M2, :] = half_grid[:, C:CP]
    rdb_s[...] = half_grid[M2 - 2 * W2 :].astype(BF)
    rdl_s[...] = half_col(0)
    rdr_s[...] = half_col(W2 - 1)
    red_rim = [
        send(rdb_s, rdt_r, at(1, 0)),
        send(rdr_s, rtl_r, at(1, 1)),
        send(rdl_s, rtr_r, at(1, -1)),
        send(rdr_s, rdl_r, at(0, 1)),
        send(rdl_s, rdr_r, at(0, -1)),
    ]
    rpf[2 : H2 + 1, 8:40, :] = half_grid.reshape(H2 - 1, W2, CP)

    arrived("y_sum", y_sum)
    total = gs[pl.ds(yy * QUART, QUART), :]
    for q in range(NY - 1):
        total = total + ry[q].astype(F32)
    zs[0:QUART, :] = total
    zs[QUART:, :] = jnp.zeros((zs.shape[0] - QUART, C), F32)
    for z in range(NZ):
        zp[z] = zs[z * PIECE : z * PIECE + PADP, :]
    zb[...] = zp[...].astype(BF)
    z_sum = [send(zb.at[lax.rem(zz + q, NZ)], rz.at[q - 1], z_peer(q)) for q in range(1, NZ)]
    arrived("bi_tx", bi_tx)
    fill_row(boo, bee, 0, not_top, birow_r[...])
    fill_cell(boo, 0, 7, not_top & not_left, bicor_r[...], HT - 1)
    for k in range(2):
        fill_row(boo, bee, 17 + k, not_bottom, biup_r[k * WT : (k + 1) * WT, :])
        fill_cell(boo, 17 + k, 7, not_bottom & not_left, bibl_r[...], k)
    gather_down(boo, bee, 0, 1, dimg, 0)
    gather_down(boo, bee, H2, 1, dimg, W2)
    half_grid = reduce(dimg)
    upper = iota((8, CP), 0) == 0
    rel_s[...] = jnp.where(upper, half_grid[0:1], half_grid[W2 : W2 + 1]).astype(BF)
    rer_s[...] = jnp.where(upper, half_grid[W2 - 1 : W2], half_grid[2 * W2 - 1 :]).astype(BF)
    red_late = [send(rer_s, rel_r, at(0, 1)), send(rel_s, rer_r, at(0, -1))]
    rpf[1, 8:40, :] = half_grid[0:W2]
    rpf[H2 + 1, 8:40, :] = keep(not_bottom, half_grid[W2:])

    arrived("red_rim", red_rim)
    rpf[0, 8:40, :] = keep(not_top, rdt_r[...].astype(F32))
    fill_col(rpf, 1, 7, not_left, rdl_r[...])
    fill_col(rpf, 1, 40, not_right, rdr_r[...])
    fill_cell(rpf, 0, 7, not_top & not_left, rtl_r[...], H2 - 1)
    fill_cell(rpf, 0, 40, not_top & not_right, rtr_r[...], H2 - 1)
    meets = (((0, 3), (1, 1)), ((1, 2), (2, 0)))

    def output_rows(pr, first, n):
        for pc in range(2):
            span = slice(2 * first + pr + 1, 2 * first + pr + 1 + 2 * n)
            plane = bee[span, 0:32, :] if pc == 0 else boo[span, 8:40, :]
            value = plane.reshape(n, 2, W2, C)[:, 0].reshape(n * W2, C)
            for di, u in meets[pr]:
                for dj, v in meets[pc]:
                    block = (u * 4 + v) * C
                    lhs = rpf[first + di : first + di + n, 7 + dj : 39 + dj, :]
                    lhs = lhs.astype(BF).reshape(n * W2, CP)
                    value = value + dot(lhs, uc[:, block : block + C])
            for k in range(n):
                start = (2 * (first + k) + pr) * WT + pc
                t32[pl.ds(start, W2, stride=2), :] = value[k * W2 : (k + 1) * W2]

    output_rows(0, 2, 6)
    output_rows(1, 1, 6)
    pay_out[3 * WT : 15 * WT, :] = t32[3 * WT : 15 * WT, :].astype(BF)
    send_output((0,))
    arrived("red_late", red_late)
    for column, flag, got in ((7, not_left, rel_r), (40, not_right, rer_r)):
        fill_cell(rpf, 1, column, flag, got[...], 0)
        fill_cell(rpf, H2 + 1, column, flag & not_bottom, got[...], 1)
    output_rows(0, 0, 2)
    output_rows(1, 0, 1)
    output_rows(1, H2 - 1, 1)
    pay_out[0 : 3 * WT, :] = t32[0 : 3 * WT, :].astype(BF)
    pay_out[15 * WT :, :] = t32[15 * WT :, :].astype(BF)
    send_output((1, 2))

    arrived("z_sum", z_sum)
    total = zp[zz]
    for q in range(NZ - 1):
        total = total + rz[q].astype(F32)
    scaling = 1.0 / math.sqrt(HT * WT * NTX * NTY)
    fin[...] = total * scaling
    last_swap = send(fin, rfin, sibling)
    arrived("last_swap", [last_swap])
    mine, other = fin[...], rfin[...]
    first = core == 0
    head = iota((16, C), 1) < 64
    for out, value in ((down_out, jnp.where(first, mine, other)), (up_out, jnp.where(first, other, mine))):
        fs[...] = pltpu.roll(value, 64, 1)
        second_half = jnp.where(head, fs[13:29, :], fs[14:30, :])
        half = jnp.where(first, value[0:16], second_half)
        for r in range(13):
            out[0:1, r * C : (r + 1) * C] = half[r : r + 1, :]
        out[0:1, 13 * C : 13 * C + 64] = half[13:14, 0:64]

    with jax.named_scope("await_blocks"):
        for pair in out_copies:
            for copy in pair:
                copy.wait_recv()
    for pair in out_copies:
        for copy in pair:
            copy.wait_send()
    for copy in started:
        copy.wait_send()


def finish(left_h, right_h, down_h, up_h, act_o, grad_o, partner_o, down_o, up_o,
           left, right, down, up, blank, isem, osem):
    seg = lax.axis_index("segment")
    even = lax.rem(seg, 2) == 0
    bring = [
        pltpu.make_async_copy(src, dst, isem.at[i])
        for i, (src, dst) in enumerate(((left_h, left), (right_h, right), (down_h, down), (up_h, up)))
    ]
    for copy in bring:
        copy.start()

    @pl.when((seg == 0) | (seg == NSEG - 1))
    def _():
        blank[...] = jnp.zeros_like(blank)

    ends = [
        pltpu.make_async_copy(left, act_o, osem.at[0]),
        pltpu.make_async_copy(right, grad_o, osem.at[1]),
        pltpu.make_async_copy(left, partner_o, osem.at[2]),
        pltpu.make_async_copy(down, down_o, osem.at[3]),
        pltpu.make_async_copy(up, up_o, osem.at[4]),
    ]

    @pl.when(seg == 0)
    def _():
        pltpu.make_async_copy(blank, act_o, osem.at[0]).start()

    @pl.when(seg == NSEG - 1)
    def _():
        pltpu.make_async_copy(blank, grad_o, osem.at[1]).start()

    for copy in bring:
        copy.wait()

    @pl.when(seg > 0)
    def _():
        ends[0].start()

    @pl.when(seg < NSEG - 1)
    def _():
        ends[1].start()

    @pl.when(even)
    def _():
        ends[2].start()

    @pl.when(jnp.logical_not(even))
    def _():
        pltpu.make_async_copy(right, partner_o, osem.at[2]).start()

    ends[3].start()
    ends[4].start()
    for copy in ends:
        copy.wait()


N_COPIES = 15 + 8 + 15 + 3 + 1 + 3 + 5 + 6 + 5 + 15 + 2 + 1


def whole_step(act, par, sta, gra, dw, uw, coarse, nown, ncell, land):
    vm = pltpu.VMEM
    fine_rows = HT * WT
    scratch = [
        vm((fine_rows, C), BF), vm((fine_rows, C), BF), vm((fine_rows, C), BF), vm((fine_rows, C), BF),
        vm((9, C2, C), BF), vm((9, C2, C), BF), vm((CELLS, C), BF), vm((1, CELLS), jnp.int32),
        vm((1, CELLS), jnp.int32), vm((HT // 4, WT // 4), jnp.int32),
        vm((CP, 9 * C), BF), vm((CP, 16 * C), BF), vm((fine_rows, C), F32), vm((fine_rows, C), F32),
        vm((fine_rows, C), F32),
        vm((18, 40, C), F32), vm((18, 40, C), F32), vm((18, 40, C), F32), vm((18, 40, C), F32),
        vm((20, 40, C), F32), vm((20, 40, C), F32),
        vm((M2, 9 * C), BF), vm((M2 - W2, 9 * C), BF), vm((2 * W2, 9 * C), BF), vm((M2, 16 * C), BF),
        vm((M2, CP), BF), vm((H2 + 1, 40, CP), F32), vm((H2 + 2, 48, CP), F32), vm((2, M2, C), F32),
        vm((CP, 16 * C), F32), vm((2, 9 * C, C), F32), vm((2, ROWS, C), F32), vm((ROWS, C), F32),
        vm((448, C), F32), vm((NZ, PADP, C), F32), vm((PADP, C), F32),
        vm((fine_rows, C), BF), vm((fine_rows, C), BF),
        vm((NTY, CAP, 128), BF), vm((NTY, CAP, 128), BF), vm((NTY, CAP, C), BF), vm((NTY, CAP, C), BF),
        vm((4 * WT, C), F32), vm((WT, C), F32),
        vm((2, WT, C), BF), vm((WT, C), BF), vm((2, HT, C), BF), vm((HT, C), BF),
        vm((2, WT, C), BF), vm((WT, C), BF), vm((2, HT, C), BF), vm((HT, C), BF),
        vm((2, HT, C), BF), vm((HT, C), BF), vm((HT, C), BF), vm((HT, C), BF),
        vm((W2, CP), BF), vm((H2, CP), BF), vm((W2, CP), BF), vm((H2, CP), BF), vm((H2, CP), BF),
        vm((WT, C), BF), vm((2 * WT, C), BF), vm((HT, C), BF),
        vm((WT, C), BF), vm((2 * WT, C), BF), vm((HT, C), BF), vm((HT, C), BF), vm((HT, C), BF),
        vm((W2, CP), BF), vm((H2, CP), BF), vm((H2, CP), BF), vm((8, CP), BF), vm((8, CP), BF),
        vm((W2, CP), BF), vm((H2, CP), BF), vm((H2, CP), BF), vm((H2, CP), BF), vm((H2, CP), BF),
        vm((8, CP), BF), vm((8, CP), BF),
        vm((ROWS, C), BF), vm((ROWS, C), BF), vm((NY, QUART, C), BF), vm((NY - 1, QUART, C), BF),
        vm((NZ, PADP, C), BF), vm((NZ - 1, PADP, C), BF), vm((PADP, C), F32), vm((PADP, C), F32),
        pltpu.SemaphoreType.DMA((N_COPIES,)), pltpu.SemaphoreType.DMA((N_COPIES,)),
        pltpu.SemaphoreType.DMA((10,)),
    ]
    in_vmem = pl.BlockSpec(memory_space=pltpu.VMEM)
    return pl.pallas_call(
        kernel,
        out_shape=(
            jax.ShapeDtypeStruct((fine_rows, C), BF),
            jax.ShapeDtypeStruct((fine_rows, C), BF),
            jax.ShapeDtypeStruct((1, ROWS), F32),
            jax.ShapeDtypeStruct((1, ROWS), F32),
        ),
        in_specs=[pl.BlockSpec(memory_space=pl.ANY)] * 10,
        out_specs=(
            pl.BlockSpec(memory_space=pl.ANY), pl.BlockSpec(memory_space=pl.ANY), in_vmem, in_vmem,
        ),
        scratch_shapes=scratch,
        compiler_params=pltpu.CompilerParams(
            collective_id=0, has_side_effects=True, vmem_limit_bytes=56 << 20
        ),
        name="relay",
    )(act, par, sta, gra, dw, uw, coarse, nown, ncell, land)


def local(
    act_in, partner_in, stashed, grad_in, down_weights, up_weights, coarse, nest_owner, nest_cell,
    land_weight,
):
    flat = (HT * WT, C)
    from_before, from_after, down_sum, up_sum = whole_step(
        act_in.reshape(flat), partner_in.reshape(flat), stashed.reshape(flat), grad_in.reshape(flat),
        jnp.swapaxes(down_weights, 3, 4).reshape(9, C2, C), up_weights.reshape(9, C2, C), coarse,
        nest_owner.reshape(1, CELLS),
        nest_cell.reshape(1, CELLS), land_weight,
    )
    block = jax.ShapeDtypeStruct(flat, BF)
    sums = jax.ShapeDtypeStruct((1, ROWS), F32)
    anywhere = pl.BlockSpec(memory_space=pl.ANY)
    act_out, grad_out, partner_out, down_sum, up_sum = pl.pallas_call(
        finish,
        out_shape=(block, block, block, sums, sums),
        in_specs=[anywhere] * 4,
        out_specs=(anywhere,) * 5,
        scratch_shapes=[
            pltpu.VMEM(flat, BF), pltpu.VMEM(flat, BF), pltpu.VMEM((1, ROWS), F32),
            pltpu.VMEM((1, ROWS), F32), pltpu.VMEM(flat, BF),
            pltpu.SemaphoreType.DMA((4,)), pltpu.SemaphoreType.DMA((5,)),
        ],
        name="finish",
    )(from_before, from_after, down_sum, up_sum)
    tile = (1, HT, WT, C)
    return (
        act_out.reshape(tile), grad_out.reshape(tile), partner_out.reshape(tile), down_sum, up_sum,
    )


def solution(mesh):
    placed = (
        P("segment", "tx", "ty", None),
        P("segment", "tx", "ty", None),
        P("segment", "tx", "ty", None),
        P("segment", "tx", "ty", None),
        P("segment", None, None, None, None),
        P("segment", None, None, None, None),
        P(("tx", "ty"), None),
        P(("tx", "ty"), None),
        P(("tx", "ty")),
        P("tx", "ty"),
    )
    return jax.shard_map(
        local,
        mesh=mesh,
        in_specs=placed,
        out_specs=(
            P("segment", "tx", "ty", None),
            P("segment", "tx", "ty", None),
            P("segment", "tx", "ty", None),
            P("segment", ("tx", "ty")),
            P("segment", ("tx", "ty")),
        ),
        check_vma=False,
    )
```

```python
import functools
import math

import jax
import jax.numpy as jnp
from jax import lax
from jax.experimental import pallas as pl
from jax.experimental.pallas import tpu as pltpu
from jax.sharding import PartitionSpec as P

F32 = jnp.float32
BF = jnp.bfloat16
MESH = pl.DeviceIdType.MESH

HT, WT, C, C2 = 16, 64, 128, 192
CP = 256
H2, W2 = HT // 2, WT // 2
M2 = H2 * W2
CELLS, CAP = 64, 8
NSEG, NTX, NTY = 4, 8, 16
NY, NZ = 4, 16
ROWS = 1728
QUART = ROWS // NY
PIECE = QUART // NZ
PADP = 32
FAR_FIRST = (8, 7, 9, 6, 10, 5, 11, 4, 12, 3, 13, 2, 14, 1, 15)
TAPS_OF = ((2,), (1, 2), (0, 1), (0,))


def dot(a, b, dims=((1,), (0,))):
    return lax.dot_general(a, b, (dims, ((), ())), preferred_element_type=F32)


def rows_of(view, index):
    lanes = view.shape[-1]
    pairs = view.reshape(view.shape[0] // 2, 2, W2, lanes)
    start = index // 2
    return pairs[start : start + H2, index % 2].reshape(M2, lanes)


def kernel(
    act_h, par_h, sta_h, gra_h, dw_h, uw_h, coarse_h, nown_h, ncell_h, land_h,
    left_out, right_out, down_out, up_out,
    act, par, sta, gra, dw, uw, coarse, nown, ncell, land,
    dwp, uc, t32, g32, b32, soo, see, goo, gee, boo, bee, dim, dimf, dimg, dimh, wim, wimg,
    pgf, rpf, r32, pw, gds, gf, gs, zs, zp, fs,
    pay_ig, pay_out,
    rqs, rqr, rps, rpr, condb, tr,
    srow_s, ogup_s, colr_s, coll_s,
    top_r, bot_r, lft_r, rgt_r, ctl_r, ctr_r, cbl_r, cbr_r,
    pgrow_s, pgcol_s, pgrow_r, pgcol_r, pgcor_r,
    birow_s, biup_s, bicol_s, birow_r, biup_r, bicol_r, bicor_r, bibl_r,
    rdb_s, rdl_s, rdr_s, rel_s, rer_s,
    rdt_r, rdl_r, rdr_r, rtl_r, rtr_r, rel_r, rer_r,
    gb, ra, yb, ry, zb, rz, fin, rfin,
    ssem, rsem, isem,
):
    seg, tx, ty = lax.axis_index("segment"), lax.axis_index("tx"), lax.axis_index("ty")
    core = lax.rem(ty, 2)
    zl = ty // 2
    zh = lax.rem(tx, 2)
    yy = tx // 2
    zz = zh * 8 + zl

    def at(dx, dy):
        return (seg, lax.rem(tx + dx + NTX, NTX), lax.rem(ty + dy + NTY, NTY))

    def ty_peer(q):
        return (seg, tx, lax.rem(ty + q, NTY))

    def y_peer(q):
        return (seg, lax.rem(yy + q, NY) * 2 + zh, ty)

    def z_peer(q):
        z = lax.rem(zz + q, NZ)
        return (seg, yy * 2 + z // 8, lax.rem(z, 8) * 2 + core)

    sibling = (seg, tx, zl * 2 + 1 - core)
    seg_next = (lax.rem(seg + 1, NSEG), tx, ty)
    seg_prev = (lax.rem(seg + NSEG - 1, NSEG), tx, ty)

    barrier = pltpu.get_barrier_semaphore()
    around = [(1, 0), (-1, 0), (0, 1), (0, -1), (1, 1), (1, -1), (-1, 1), (-1, -1)]
    greeted = [at(dx, dy) for dx, dy in around if dx != 0]
    greeted += [ty_peer(q) for q in range(1, NTY)]
    greeted += [y_peer(q) for q in range(1, NY)]
    greeted += [z_peer(q) for q in range(1, NZ)]
    greeted += [seg_next, seg_prev]
    for device in greeted:
        pl.semaphore_signal(barrier, inc=1, device_id=device, device_id_type=MESH)

    bring = [
        pltpu.make_async_copy(src, dst, isem.at[i])
        for i, (src, dst) in enumerate((
            (nown_h, nown), (ncell_h, ncell), (land_h, land), (gra_h, gra), (par_h, par), (sta_h, sta),
            (coarse_h, coarse), (act_h, act), (uw_h, uw), (dw_h, dw),
        ))
    ]
    for copy in bring:
        copy.start()

    count = [0]
    started = []

    def slot():
        count[0] += 1
        return count[0] - 1

    def make(index, src, dst, device):
        return pltpu.make_async_remote_copy(
            src_ref=src, dst_ref=dst, send_sem=ssem.at[index], recv_sem=rsem.at[index],
            device_id=device, device_id_type=MESH,
        )

    def send(src, dst, device, goes=None, comes=None):
        copy = make(slot(), src, dst, device)
        if goes is None:
            copy.start()
        else:
            pl.when(goes)(copy.start)
        started.append((copy, goes))
        return copy, comes

    def send_right(src, dst):
        return send(src, dst, at(0, 1), not_right, not_left)

    def send_left(src, dst):
        return send(src, dst, at(0, -1), not_left, not_right)

    def arrived(name, copies):
        with jax.named_scope("await_" + name):
            for copy, comes in copies:
                if comes is None:
                    copy.wait_recv()
                else:
                    pl.when(comes)(copy.wait_recv)

    not_top, not_bottom = tx > 0, tx < NTX - 1
    not_left, not_right = ty > 0, ty < NTY - 1

    def keep(flag, value):
        return jnp.where(flag, value, 0.0)

    for copy in bring[:3]:
        copy.wait()
    decoder = (seg >= NSEG // 2).astype(F32)
    encoder = 1.0 - decoder

    def iota(shape, axis):
        return lax.broadcasted_iota(jnp.int32, shape, axis)

    orow = nown[...].astype(F32)
    crow = ncell[...].astype(F32)
    n0, n1 = iota((CELLS, CELLS), 0), iota((CELLS, CELLS), 1)
    ocol = jnp.sum(jnp.where(n0 == n1, orow, 0.0), axis=1, keepdims=True)
    ccol = jnp.sum(jnp.where(n0 == n1, crow, 0.0), axis=1, keepdims=True)
    same = jnp.where(ocol == orow, 1.0, 0.0)
    slot_row = jnp.sum(jnp.where(n0 < n1, same, 0.0), axis=0, keepdims=True)
    slot_col = jnp.sum(jnp.where(n1 < n0, same, 0.0), axis=1, keepdims=True)
    tyf = ty.astype(F32)

    def place(owner, slots):
        offset = owner - tyf
        return jnp.where(offset < 0.0, offset + NTY, offset) * CAP + slots

    qrow, qcol = place(orow, slot_row), place(ocol, slot_col)
    chosen = jnp.where(iota((NTY * CAP, CELLS), 0).astype(F32) == qrow, 1.0, 0.0).astype(BF)
    cell_hot = jnp.where(ccol == iota((CELLS, 128), 1).astype(F32), 1.0, 0.0).astype(BF)
    asked = dot(chosen, cell_hot)
    for q in range(NTY):
        rqs[q] = asked[q * CAP : (q + 1) * CAP].astype(BF)
    rqr[0] = rqs[0]

    for copy in bring[3:6]:
        copy.wait()
    spread = iota((WT, WT // 4), 1) == (iota((WT, WT // 4), 0) >> 2)
    for k in range(HT // 4):
        row = land[k : k + 1, :].astype(F32)
        weight = jnp.sum(jnp.where(spread, row, 0.0), axis=1, keepdims=True)
        weight = jnp.where(seg == NSEG - 1, weight, 1.0)
        for y in range(4 * k, 4 * k + 4):
            part = pl.ds(y * WT, WT)
            value = (gra[part, :].astype(F32) + encoder * par[part, :].astype(F32)) * weight
            g32[part, :] = value.astype(BF).astype(F32)
    t32[...] = sta[...].astype(F32)

    last = (HT - 1) * WT
    srow_s[0] = sta[last : last + WT, :]
    srow_s[1] = g32[last : last + WT, :].astype(BF)
    ogup_s[...] = g32[0:WT, :].astype(BF)
    colr_s[0] = t32[pl.ds(WT - 1, HT, stride=WT), :].astype(BF)
    colr_s[1] = g32[pl.ds(WT - 1, HT, stride=WT), :].astype(BF)
    coll_s[...] = g32[pl.ds(0, HT, stride=WT), :].astype(BF)

    with jax.named_scope("await_entry"):
        pl.semaphore_wait(barrier, len(greeted))

    rim_tx = [
        send(srow_s, top_r, at(1, 0)),
        send(ogup_s, bot_r, at(-1, 0)),
        send(colr_s, ctl_r, at(1, 1)),
        send(coll_s, ctr_r, at(1, -1)),
        send(colr_s.at[1], cbl_r, at(-1, 1)),
        send(coll_s, cbr_r, at(-1, -1)),
    ]
    request = [send(rqs.at[q], rqr.at[q], ty_peer(q)) for q in range(1, NTY)]
    rim_ty = [send_right(colr_s, lft_r), send_left(coll_s, rgt_r)]

    for copy in bring[6:]:
        copy.wait()
    dwp[C2:CP, :] = jnp.zeros((CP - C2, 9 * C), BF)
    for t in range(9):
        dwp[0:C2, t * C : (t + 1) * C] = dw[t]
    uc[C2:CP, :] = jnp.zeros((CP - C2, 16 * C), BF)
    for u in range(4):
        for v in range(4):
            total = None
            for a in TAPS_OF[u]:
                for b in TAPS_OF[v]:
                    tap = uw[a * 3 + b].astype(F32)
                    total = tap if total is None else total + tap
            block = (u * 4 + v) * C
            uc[0:C2, block : block + C] = total.astype(BF)

    def fill(oo, ee, fine):
        ee[1:17, 0:W2, :] = fine[pl.ds(0, HT * W2, stride=2), :].reshape(HT, W2, C)
        oo[1:17, 8:40, :] = fine[pl.ds(1, HT * W2, stride=2), :].reshape(HT, W2, C)

    def fill_row(oo, ee, r, flag, row):
        tr[...] = keep(flag, row.astype(F32))
        ee[r, 0:W2, :] = tr[pl.ds(0, W2, stride=2), :]
        oo[r, 8:40, :] = tr[pl.ds(1, W2, stride=2), :]

    def fill_col(plane, first, at_col, flag, column):
        values = keep(flag, column.astype(F32))
        for r in range(values.shape[0]):
            plane[first + r, at_col : at_col + 1, :] = values[r : r + 1, :]

    def fill_cell(plane, r, at_col, flag, column, i):
        values = keep(flag, column.astype(F32))
        plane[r, at_col : at_col + 1, :] = values[i : i + 1, :]

    def half_col(j):
        halves = [r32[h, pl.ds(j, H2, stride=W2), :] for h in range(2)]
        return jnp.concatenate(halves, axis=1).astype(BF)

    def gather_down(oo, ee, first, n, lhs, row):
        span = slice(2 * first, 2 * first + 2 * n + 2)
        for b, view in enumerate([oo[span, 7:39, :], ee[span, 0:32, :], oo[span, 8:40, :]]):
            pairs = view.astype(BF).reshape(n + 1, 2, W2, C)
            for a in range(3):
                block = (a * 3 + b) * C
                part = pairs[a // 2 : a // 2 + n, a % 2].reshape(n * W2, C)
                lhs[row : row + n * W2, block : block + C] = part

    fill(soo, see, t32)
    fill(goo, gee, g32)

    def gather_wide(first, n, lhs, row):
        span = slice(2 * first, 2 * first + 2 * n + 2)
        views = [goo[span, 7:39, :], gee[span, 0:32, :], goo[span, 8:40, :], gee[span, 1:33, :]]
        for v, view in enumerate(views):
            pairs = view.astype(BF).reshape(n + 1, 2, W2, C)
            for u in range(4):
                block = (u * 4 + v) * C
                part = pairs[u // 2 : u // 2 + n, u % 2].reshape(n * W2, C)
                lhs[row : row + n * W2, block : block + C] = part

    def backward(narrow, wide):
        pre_back = dot(narrow[...], dwp[...], ((1,), (1,)))
        gate = jax.nn.sigmoid(pre_back)
        raised = (pre_back * gate).astype(BF)
        pooled = dot(wide[...], uc[...], ((1,), (1,)))
        pre_grad = (pooled * (gate * (1.0 + pre_back * (1.0 - gate)))).astype(BF)
        down_part = dot(narrow[...], pre_grad, ((0,), (0,)))
        up_part = dot(raised, wide[...], ((0,), (0,)))
        return pre_grad.astype(F32), down_part, up_part

    def put_half(value, row):
        r32[0, row : row + value.shape[0], :] = value[:, 0:C]
        r32[1, row : row + value.shape[0], :] = value[:, C:CP]

    arrived("rim_ty", rim_ty)
    fill_col(soo, 1, 7, not_left, lft_r[0])
    fill_col(goo, 1, 7, not_left, lft_r[1])
    fill_col(gee, 1, W2, not_right, rgt_r[...])
    gather_down(soo, see, 1, H2 - 2, dim, 0)
    gather_wide(1, H2 - 2, wim, 0)
    inner, down_part, up_part = backward(dim, wim)
    put_half(inner, W2)
    pgf[1 : H2 - 1, 0:W2, :] = inner.reshape(H2 - 2, W2, CP)
    gds[0] = down_part[:, 0:C]
    gds[1] = down_part[:, C:CP]
    pw[...] = up_part

    arrived("request", request)
    wanted = jnp.concatenate([rqr[q].astype(F32) for q in range(NTY)], axis=0)
    answer = dot(wanted[:, 0:CELLS].astype(BF), coarse[...])
    for q in range(NTY):
        rps[q] = answer[q * CAP : (q + 1) * CAP].astype(BF)
    rpr[0] = rps[0]
    reply = [
        send(rps.at[q], rpr.at[q], (seg, tx, lax.rem(ty + NTY - q, NTY))) for q in range(1, NTY)
    ]

    arrived("rim_tx", rim_tx)
    fill_row(soo, see, 0, not_top, top_r[0])
    fill_row(goo, gee, 0, not_top, top_r[1])
    fill_row(goo, gee, 17, not_bottom, bot_r[...])
    fill_cell(soo, 0, 7, not_top & not_left, ctl_r[0], HT - 1)
    fill_cell(goo, 0, 7, not_top & not_left, ctl_r[1], HT - 1)
    fill_cell(gee, 0, W2, not_top & not_right, ctr_r[...], HT - 1)
    fill_cell(goo, 17, 7, not_bottom & not_left, cbl_r[...], 0)
    fill_cell(gee, 17, W2, not_bottom & not_right, cbr_r[...], 0)
    for first, row in ((0, 0), (H2 - 1, W2)):
        gather_down(soo, see, first, 1, dimg, row)
        gather_wide(first, 1, wimg, row)
    outer, down_part, up_part = backward(dimg, wimg)
    put_half(outer[0:W2], 0)
    put_half(outer[W2:], M2 - W2)
    pgrow_s[...] = outer[0:W2].astype(BF)
    pgcol_s[...] = half_col(0)
    pg_rim = [
        send(pgrow_s, pgrow_r, at(-1, 0)),
        send(pgcol_s, pgcor_r, at(-1, -1)),
        send_left(pgcol_s, pgcol_r),
    ]
    pgf[0, 0:W2, :] = outer[0:W2]
    pgf[H2 - 1, 0:W2, :] = outer[W2:]
    gds[0] = gds[0] + down_part[:, 0:C]
    gds[1] = gds[1] + down_part[:, C:CP]
    pw[...] = pw[...] + up_part

    low = iota((ROWS // 3, C), 1) < 64
    even_lo = gds[0, pl.ds(0, ROWS // 3, stride=2), :]
    even_hi = gds[1, pl.ds(0, ROWS // 3, stride=2), :]
    odd_lo = pltpu.roll(gds[0, pl.ds(1, ROWS // 3, stride=2), :], 64, 1)
    odd_hi = pltpu.roll(gds[1, pl.ds(1, ROWS // 3, stride=2), :], 64, 1)
    gf[0, pl.ds(0, ROWS // 3, stride=3), :] = even_lo
    gf[0, pl.ds(1, ROWS // 3, stride=3), :] = jnp.where(low, even_hi, odd_lo)
    gf[0, pl.ds(2, ROWS // 3, stride=3), :] = jnp.where(low, odd_lo, odd_hi)
    for a in range(3):
        for b in range(3):
            total = None
            for u in (2 - a, 3 - a):
                for v in (2 - b, 3 - b):
                    block = (u * 4 + v) * C
                    term = pw[0:C2, block : block + C]
                    total = term if total is None else total + term
            tap = (a * 3 + b) * C2
            gf[1, tap : tap + C2, :] = total
    gb[...] = gf[1 - core].astype(BF)
    swap = send(gb, ra, sibling)

    arrived("swap", [swap])
    gs[...] = gf[core] + ra[...].astype(F32)
    yb[...] = gs[...].astype(BF).reshape(NY, QUART, C)
    y_sum = [send(yb.at[lax.rem(yy + q, NY)], ry.at[q - 1], y_peer(q)) for q in (2, 1, 3)]

    arrived("reply", reply)
    table = jnp.concatenate([rpr[q].astype(F32) for q in range(NTY)], axis=0).astype(BF)
    pick = jnp.where(iota((CELLS, NTY * CAP), 1).astype(F32) == qcol, 1.0, 0.0).astype(BF)
    fetched = dot(pick, table).astype(BF)
    r0, r1 = iota((4 * WT, CELLS), 0), iota((4 * WT, CELLS), 1)
    widen = jnp.where(r1 == ((r0 >> 6) << 4) + ((r0 & 63) >> 2), 1.0, 0.0).astype(BF)
    condb[...] = dot(widen, fetched)
    for y in range(HT):
        part = pl.ds(y * WT, WT)
        value = (
            act[part, :].astype(F32)
            + decoder * par[part, :].astype(F32)
            + condb[pl.ds(y // 4 * WT, WT), :]
        )
        b32[part, :] = value.astype(BF).astype(F32)
    birow_s[...] = b32[last : last + WT, :].astype(BF)
    bicol_s[...] = b32[pl.ds(WT - 1, HT, stride=WT), :].astype(BF)
    biup_s[...] = b32[0 : 2 * WT, :].astype(BF)
    bi_tx = [
        send(birow_s, birow_r, at(1, 0)),
        send(biup_s, biup_r, at(-1, 0)),
        send(bicol_s, bicor_r, at(1, 1)),
        send(bicol_s, bibl_r, at(-1, 1)),
    ]
    bi_ty = [send_right(bicol_s, bicol_r)]
    fill(boo, bee, b32)

    def reduce(lhs):
        pre_down = dot(lhs[...], dwp[...], ((1,), (1,)))
        return (pre_down * jax.nn.sigmoid(pre_down)).astype(BF).astype(F32)

    arrived("bi_ty", bi_ty)
    fill_col(boo, 1, 7, not_left, bicol_r[...])
    gather_down(boo, bee, 1, H2 - 1, dimf, 0)
    half_grid = reduce(dimf)
    r32[0, W2:M2, :] = half_grid[:, 0:C]
    r32[1, W2:M2, :] = half_grid[:, C:CP]
    rdb_s[...] = half_grid[M2 - 2 * W2 :].astype(BF)
    rdl_s[...] = half_col(0)
    rdr_s[...] = half_col(W2 - 1)
    red_tx = [
        send(rdb_s, rdt_r, at(1, 0)),
        send(rdr_s, rtl_r, at(1, 1)),
        send(rdl_s, rtr_r, at(1, -1)),
    ]
    red_ty = [send_right(rdr_s, rdl_r), send_left(rdl_s, rdr_r)]
    rpf[2 : H2 + 1, 8:40, :] = half_grid.reshape(H2 - 1, W2, CP)

    parts = [pl.ds(3 * WT, 12 * WT), pl.ds(0, 3 * WT), pl.ds(15 * WT, WT)]
    slots = [(slot(), slot()) for _ in parts]

    def block_copies(source):
        return [
            (make(up, source.at[part, :], left_out.at[part, :], seg_next),
             make(down, source.at[part, :], right_out.at[part, :], seg_prev))
            for part, (up, down) in zip(parts, slots)
        ]

    ig_copies, out_copies = block_copies(pay_ig), block_copies(pay_out)

    def send_output(which):
        @pl.when(seg <= NSEG - 2)
        def _():
            for k in which:
                out_copies[k][0].start()

        @pl.when(seg == 0)
        def _():
            for k in which:
                out_copies[k][1].start()

    arrived("red_ty", red_ty)
    fill_col(rpf, 1, 7, not_left, rdl_r[...])
    fill_col(rpf, 1, 40, not_right, rdr_r[...])
    meets = (((0, 3), (1, 1)), ((1, 2), (2, 0)))

    def output_rows(pr, first, n):
        for pc in range(2):
            span = slice(2 * first + pr + 1, 2 * first + pr + 1 + 2 * n)
            plane = bee[span, 0:32, :] if pc == 0 else boo[span, 8:40, :]
            value = plane.reshape(n, 2, W2, C)[:, 0].reshape(n * W2, C)
            for di, u in meets[pr]:
                for dj, v in meets[pc]:
                    block = (u * 4 + v) * C
                    lhs = rpf[first + di : first + di + n, 7 + dj : 39 + dj, :]
                    lhs = lhs.astype(BF).reshape(n * W2, CP)
                    value = value + dot(lhs, uc[:, block : block + C])
            for k in range(n):
                start = (2 * (first + k) + pr) * WT + pc
                t32[pl.ds(start, W2, stride=2), :] = value[k * W2 : (k + 1) * W2]

    output_rows(0, 2, 6)
    output_rows(1, 1, 6)
    pay_out[3 * WT : 15 * WT, :] = t32[3 * WT : 15 * WT, :].astype(BF)
    send_output((0,))
    arrived("y_sum", y_sum)
    total = gs[pl.ds(yy * QUART, QUART), :]
    for q in range(NY - 1):
        total = total + ry[q].astype(F32)
    zs[0:QUART, :] = total
    zs[QUART:, :] = jnp.zeros((zs.shape[0] - QUART, C), F32)
    for z in range(NZ):
        zp[z] = zs[z * PIECE : z * PIECE + PADP, :]
    zb[...] = zp[...].astype(BF)
    z_sum = [send(zb.at[lax.rem(zz + q, NZ)], rz.at[q - 1], z_peer(q)) for q in FAR_FIRST]
    arrived("pg_rim", pg_rim)
    pgf[H2, 0:W2, :] = keep(not_bottom, pgrow_r[...].astype(F32))
    fill_col(pgf, 0, W2, not_right, pgcol_r[...])
    fill_cell(pgf, H2, W2, not_bottom & not_right, pgcor_r[...], 0)
    shifted = [
        [pgf[di : di + H2, dj : dj + W2, :].astype(BF).reshape(M2, CP) for dj in (0, 1)]
        for di in (0, 1)
    ]

    def spread_out(value, pr, pc):
        for i in range(H2):
            t32[pl.ds((2 * i + pr) * WT + pc, W2, stride=2), :] = value[i * W2 : (i + 1) * W2]

    for pr in range(2):
        for pc in range(2):
            plane = gee[:, 0:32, :] if pc == 0 else goo[:, 8:40, :]
            value = rows_of(plane, 1 + pr)
            for a, di in ((1, 0),) if pr == 0 else ((2, 0), (0, 1)):
                for b, dj in ((1, 0),) if pc == 0 else ((2, 0), (0, 1)):
                    tap = (a * 3 + b) * C
                    value = value + dot(shifted[di][dj], dwp[:, tap : tap + C])
            spread_out(value, pr, pc)
    pay_ig[...] = t32[...].astype(BF)

    @pl.when(seg == NSEG - 1)
    def _():
        for copy, _ in ig_copies:
            copy.start()

    @pl.when(seg >= 1)
    def _():
        for _, copy in ig_copies:
            copy.start()

    arrived("bi_tx", bi_tx)
    fill_row(boo, bee, 0, not_top, birow_r[...])
    fill_cell(boo, 0, 7, not_top & not_left, bicor_r[...], HT - 1)
    for k in range(2):
        fill_row(boo, bee, 17 + k, not_bottom, biup_r[k * WT : (k + 1) * WT, :])
        fill_cell(boo, 17 + k, 7, not_bottom & not_left, bibl_r[...], k)
    gather_down(boo, bee, 0, 1, dimh, 0)
    gather_down(boo, bee, H2, 1, dimh, W2)
    half_grid = reduce(dimh)
    upper = iota((8, CP), 0) == 0
    rel_s[...] = jnp.where(upper, half_grid[0:1], half_grid[W2 : W2 + 1]).astype(BF)
    rer_s[...] = jnp.where(upper, half_grid[W2 - 1 : W2], half_grid[2 * W2 - 1 :]).astype(BF)
    red_late = [send_right(rer_s, rel_r), send_left(rel_s, rer_r)]
    rpf[1, 8:40, :] = half_grid[0:W2]
    rpf[H2 + 1, 8:40, :] = keep(not_bottom, half_grid[W2:])

    arrived("red_tx", red_tx)
    rpf[0, 8:40, :] = keep(not_top, rdt_r[...].astype(F32))
    fill_cell(rpf, 0, 7, not_top & not_left, rtl_r[...], H2 - 1)
    fill_cell(rpf, 0, 40, not_top & not_right, rtr_r[...], H2 - 1)
    arrived("red_late", red_late)
    for column, flag, got in ((7, not_left, rel_r), (40, not_right, rer_r)):
        fill_cell(rpf, 1, column, flag, got[...], 0)
        fill_cell(rpf, H2 + 1, column, flag & not_bottom, got[...], 1)
    output_rows(0, 0, 2)
    output_rows(1, 0, 1)
    output_rows(1, H2 - 1, 1)
    pay_out[0 : 3 * WT, :] = t32[0 : 3 * WT, :].astype(BF)
    pay_out[15 * WT :, :] = t32[15 * WT :, :].astype(BF)
    send_output((1, 2))

    arrived("z_sum", z_sum)
    total = zp[zz]
    for q in range(NZ - 1):
        total = total + rz[q].astype(F32)
    scaling = 1.0 / math.sqrt(HT * WT * NTX * NTY)
    fin[...] = total * scaling
    last_swap = send(fin, rfin, sibling)
    arrived("last_swap", [last_swap])
    mine, other = fin[...], rfin[...]
    first = core == 0
    head = iota((16, C), 1) < 64
    for out, value in ((down_out, jnp.where(first, mine, other)), (up_out, jnp.where(first, other, mine))):
        fs[...] = pltpu.roll(value, 64, 1)
        second_half = jnp.where(head, fs[13:29, :], fs[14:30, :])
        half = jnp.where(first, value[0:16], second_half)
        for r in range(13):
            out[0:1, r * C : (r + 1) * C] = half[r : r + 1, :]
        out[0:1, 13 * C : 13 * C + 64] = half[13:14, 0:64]

    with jax.named_scope("await_blocks"):
        for pair in out_copies:
            for copy in pair:
                copy.wait_recv()
    for pair in out_copies:
        for copy in pair:
            copy.wait_send()
    for copy, goes in started:
        if goes is None:
            copy.wait_send()
        else:
            pl.when(goes)(copy.wait_send)


def finish(left_h, right_h, down_h, up_h, act_o, grad_o, partner_o, down_o, up_o,
           left, right, down, up, blank, isem, osem):
    seg = lax.axis_index("segment")
    even = lax.rem(seg, 2) == 0
    bring = [
        pltpu.make_async_copy(src, dst, isem.at[i])
        for i, (src, dst) in enumerate(((left_h, left), (right_h, right), (down_h, down), (up_h, up)))
    ]
    for copy in bring:
        copy.start()

    @pl.when((seg == 0) | (seg == NSEG - 1))
    def _():
        blank[...] = jnp.zeros_like(blank)

    ends = [
        pltpu.make_async_copy(left, act_o, osem.at[0]),
        pltpu.make_async_copy(right, grad_o, osem.at[1]),
        pltpu.make_async_copy(left, partner_o, osem.at[2]),
        pltpu.make_async_copy(down, down_o, osem.at[3]),
        pltpu.make_async_copy(up, up_o, osem.at[4]),
    ]

    @pl.when(seg == 0)
    def _():
        pltpu.make_async_copy(blank, act_o, osem.at[0]).start()

    @pl.when(seg == NSEG - 1)
    def _():
        pltpu.make_async_copy(blank, grad_o, osem.at[1]).start()

    for copy in bring:
        copy.wait()

    @pl.when(seg > 0)
    def _():
        ends[0].start()

    @pl.when(seg < NSEG - 1)
    def _():
        ends[1].start()

    @pl.when(even)
    def _():
        ends[2].start()

    @pl.when(jnp.logical_not(even))
    def _():
        pltpu.make_async_copy(right, partner_o, osem.at[2]).start()

    ends[3].start()
    ends[4].start()
    for copy in ends:
        copy.wait()


N_COPIES = 15 + 8 + 15 + 3 + 1 + 3 + 5 + 6 + 5 + 15 + 2 + 1


def whole_step(act, par, sta, gra, dw, uw, coarse, nown, ncell, land):
    vm = pltpu.VMEM
    fine_rows = HT * WT
    scratch = [
        vm((fine_rows, C), BF), vm((fine_rows, C), BF), vm((fine_rows, C), BF), vm((fine_rows, C), BF),
        vm((9, C2, C), BF), vm((9, C2, C), BF), vm((CELLS, C), BF), vm((1, CELLS), jnp.int32),
        vm((1, CELLS), jnp.int32), vm((HT // 4, WT // 4), jnp.int32),
        vm((CP, 9 * C), BF), vm((CP, 16 * C), BF), vm((fine_rows, C), F32), vm((fine_rows, C), F32),
        vm((fine_rows, C), F32),
        vm((18, 40, C), F32), vm((18, 40, C), F32), vm((18, 40, C), F32), vm((18, 40, C), F32),
        vm((20, 40, C), F32), vm((20, 40, C), F32),
        vm((M2 - 2 * W2, 9 * C), BF), vm((M2 - W2, 9 * C), BF), vm((2 * W2, 9 * C), BF),
        vm((2 * W2, 9 * C), BF), vm((M2 - 2 * W2, 16 * C), BF), vm((2 * W2, 16 * C), BF),
        vm((H2 + 1, 40, CP), F32), vm((H2 + 2, 48, CP), F32), vm((2, M2, C), F32),
        vm((CP, 16 * C), F32), vm((2, 9 * C, C), F32), vm((2, ROWS, C), F32), vm((ROWS, C), F32),
        vm((448, C), F32), vm((NZ, PADP, C), F32), vm((PADP, C), F32),
        vm((fine_rows, C), BF), vm((fine_rows, C), BF),
        vm((NTY, CAP, 128), BF), vm((NTY, CAP, 128), BF), vm((NTY, CAP, C), BF), vm((NTY, CAP, C), BF),
        vm((4 * WT, C), F32), vm((WT, C), F32),
        vm((2, WT, C), BF), vm((WT, C), BF), vm((2, HT, C), BF), vm((HT, C), BF),
        vm((2, WT, C), BF), vm((WT, C), BF), vm((2, HT, C), BF), vm((HT, C), BF),
        vm((2, HT, C), BF), vm((HT, C), BF), vm((HT, C), BF), vm((HT, C), BF),
        vm((W2, CP), BF), vm((H2, CP), BF), vm((W2, CP), BF), vm((H2, CP), BF), vm((H2, CP), BF),
        vm((WT, C), BF), vm((2 * WT, C), BF), vm((HT, C), BF),
        vm((WT, C), BF), vm((2 * WT, C), BF), vm((HT, C), BF), vm((HT, C), BF), vm((HT, C), BF),
        vm((W2, CP), BF), vm((H2, CP), BF), vm((H2, CP), BF), vm((8, CP), BF), vm((8, CP), BF),
        vm((W2, CP), BF), vm((H2, CP), BF), vm((H2, CP), BF), vm((H2, CP), BF), vm((H2, CP), BF),
        vm((8, CP), BF), vm((8, CP), BF),
        vm((ROWS, C), BF), vm((ROWS, C), BF), vm((NY, QUART, C), BF), vm((NY - 1, QUART, C), BF),
        vm((NZ, PADP, C), BF), vm((NZ - 1, PADP, C), BF), vm((PADP, C), F32), vm((PADP, C), F32),
        pltpu.SemaphoreType.DMA((N_COPIES,)), pltpu.SemaphoreType.DMA((N_COPIES,)),
        pltpu.SemaphoreType.DMA((10,)),
    ]
    in_vmem = pl.BlockSpec(memory_space=pltpu.VMEM)
    return pl.pallas_call(
        kernel,
        out_shape=(
            jax.ShapeDtypeStruct((fine_rows, C), BF),
            jax.ShapeDtypeStruct((fine_rows, C), BF),
            jax.ShapeDtypeStruct((1, ROWS), F32),
            jax.ShapeDtypeStruct((1, ROWS), F32),
        ),
        in_specs=[pl.BlockSpec(memory_space=pl.ANY)] * 10,
        out_specs=(
            pl.BlockSpec(memory_space=pl.ANY), pl.BlockSpec(memory_space=pl.ANY), in_vmem, in_vmem,
        ),
        scratch_shapes=scratch,
        compiler_params=pltpu.CompilerParams(
            collective_id=0, has_side_effects=True, vmem_limit_bytes=56 << 20
        ),
        name="relay",
    )(act, par, sta, gra, dw, uw, coarse, nown, ncell, land)


def local(
    act_in, partner_in, stashed, grad_in, down_weights, up_weights, coarse, nest_owner, nest_cell,
    land_weight,
):
    flat = (HT * WT, C)
    from_before, from_after, down_sum, up_sum = whole_step(
        act_in.reshape(flat), partner_in.reshape(flat), stashed.reshape(flat), grad_in.reshape(flat),
        jnp.swapaxes(down_weights, 3, 4).reshape(9, C2, C), up_weights.reshape(9, C2, C), coarse,
        nest_owner.reshape(1, CELLS),
        nest_cell.reshape(1, CELLS), land_weight,
    )
    block = jax.ShapeDtypeStruct(flat, BF)
    sums = jax.ShapeDtypeStruct((1, ROWS), F32)
    anywhere = pl.BlockSpec(memory_space=pl.ANY)
    act_out, grad_out, partner_out, down_sum, up_sum = pl.pallas_call(
        finish,
        out_shape=(block, block, block, sums, sums),
        in_specs=[anywhere] * 4,
        out_specs=(anywhere,) * 5,
        scratch_shapes=[
            pltpu.VMEM(flat, BF), pltpu.VMEM(flat, BF), pltpu.VMEM((1, ROWS), F32),
            pltpu.VMEM((1, ROWS), F32), pltpu.VMEM(flat, BF),
            pltpu.SemaphoreType.DMA((4,)), pltpu.SemaphoreType.DMA((5,)),
        ],
        name="finish",
    )(from_before, from_after, down_sum, up_sum)
    tile = (1, HT, WT, C)
    return (
        act_out.reshape(tile), grad_out.reshape(tile), partner_out.reshape(tile), down_sum, up_sum,
    )


def solution(mesh):
    placed = (
        P("segment", "tx", "ty", None),
        P("segment", "tx", "ty", None),
        P("segment", "tx", "ty", None),
        P("segment", "tx", "ty", None),
        P("segment", None, None, None, None),
        P("segment", None, None, None, None),
        P(("tx", "ty"), None),
        P(("tx", "ty"), None),
        P(("tx", "ty")),
        P("tx", "ty"),
    )
    return jax.shard_map(
        local,
        mesh=mesh,
        in_specs=placed,
        out_specs=(
            P("segment", "tx", "ty", None),
            P("segment", "tx", "ty", None),
            P("segment", "tx", "ty", None),
            P("segment", ("tx", "ty")),
            P("segment", ("tx", "ty")),
        ),
        check_vma=False,
    )
```

```python
import functools
import math

import jax
import jax.numpy as jnp
from jax import lax
from jax.experimental import pallas as pl
from jax.experimental.pallas import tpu as pltpu
from jax.sharding import PartitionSpec as P

F32 = jnp.float32
BF = jnp.bfloat16
MESH = pl.DeviceIdType.MESH

HT, WT, C, C2 = 16, 64, 128, 192
CP = 256
H2, W2 = HT // 2, WT // 2
M2 = H2 * W2
CELLS, CAP = 64, 8
NSEG, NTX, NTY = 4, 8, 16
NY, NZ = 4, 16
ROWS = 1728
QUART = ROWS // NY
PIECE = QUART // NZ
PADP = 32
FAR_FIRST = (8, 7, 9, 6, 10, 5, 11, 4, 12, 3, 13, 2, 14, 1, 15)
TAPS_OF = ((2,), (1, 2), (0, 1), (0,))


def dot(a, b, dims=((1,), (0,))):
    return lax.dot_general(a, b, (dims, ((), ())), preferred_element_type=F32)


def rows_of(view, index):
    lanes = view.shape[-1]
    pairs = view.reshape(view.shape[0] // 2, 2, W2, lanes)
    start = index // 2
    return pairs[start : start + H2, index % 2].reshape(M2, lanes)


def kernel(
    act_h, par_h, sta_h, gra_h, dw_h, uw_h, coarse_h, nown_h, ncell_h, land_h,
    left_out, right_out, down_out, up_out,
    act, par, sta, gra, dw, uw, coarse, nown, ncell, land,
    dwp, uc, t32, g32, b32, soo, see, goo, gee, boo, bee, dim, dimf, dimg, dimh, wim, wimg,
    pgf, rpf, r32, pw, gds, gf, gs, zs, zp, fs,
    pay_ig, pay_out,
    rqs, rqr, rps, rpr, condb, tr,
    srow_s, ogup_s, colr_s, coll_s,
    top_r, bot_r, lft_r, rgt_r, ctl_r, ctr_r, cbl_r, cbr_r,
    pgrow_s, pgcol_s, pgrow_r, pgcol_r, pgcor_r,
    birow_s, biup_s, bicol_s, birow_r, biup_r, bicol_r, bicor_r, bibl_r,
    rdb_s, rdl_s, rdr_s, rel_s, rer_s,
    rdt_r, rdl_r, rdr_r, rtl_r, rtr_r, rel_r, rer_r,
    gb, ra, yb, ry, zb, rz, fin, rfin,
    ssem, rsem, isem,
):
    seg, tx, ty = lax.axis_index("segment"), lax.axis_index("tx"), lax.axis_index("ty")
    core = lax.rem(ty, 2)
    zl = ty // 2
    zh = lax.rem(tx, 2)
    yy = tx // 2
    zz = zh * 8 + zl

    def at(dx, dy):
        return (seg, lax.rem(tx + dx + NTX, NTX), lax.rem(ty + dy + NTY, NTY))

    def ty_peer(q):
        return (seg, tx, lax.rem(ty + q, NTY))

    def y_peer(q):
        return (seg, lax.rem(yy + q, NY) * 2 + zh, ty)

    def z_peer(q):
        z = lax.rem(zz + q, NZ)
        return (seg, yy * 2 + z // 8, lax.rem(z, 8) * 2 + core)

    sibling = (seg, tx, zl * 2 + 1 - core)
    seg_next = (lax.rem(seg + 1, NSEG), tx, ty)
    seg_prev = (lax.rem(seg + NSEG - 1, NSEG), tx, ty)

    barrier = pltpu.get_barrier_semaphore()
    around = [(1, 0), (-1, 0), (0, 1), (0, -1), (1, 1), (1, -1), (-1, 1), (-1, -1)]
    greeted = [at(dx, dy) for dx, dy in around if dx != 0]
    greeted += [ty_peer(q) for q in range(1, NTY)]
    greeted += [y_peer(q) for q in range(1, NY)]
    greeted += [z_peer(q) for q in range(1, NZ)]
    greeted += [seg_next, seg_prev]
    for device in greeted:
        pl.semaphore_signal(barrier, inc=1, device_id=device, device_id_type=MESH)

    bring = [
        pltpu.make_async_copy(src, dst, isem.at[i])
        for i, (src, dst) in enumerate((
            (nown_h, nown), (ncell_h, ncell), (land_h, land), (gra_h, gra), (par_h, par), (sta_h, sta),
            (coarse_h, coarse), (act_h, act), (uw_h, uw), (dw_h, dw),
        ))
    ]
    for copy in bring:
        copy.start()

    count = [0]
    started = []

    def slot():
        count[0] += 1
        return count[0] - 1

    def make(index, src, dst, device):
        return pltpu.make_async_remote_copy(
            src_ref=src, dst_ref=dst, send_sem=ssem.at[index], recv_sem=rsem.at[index],
            device_id=device, device_id_type=MESH,
        )

    def send(src, dst, device, goes=None, comes=None):
        copy = make(slot(), src, dst, device)
        if goes is None:
            copy.start()
        else:
            pl.when(goes)(copy.start)
        started.append((copy, goes))
        return copy, comes

    def send_right(src, dst):
        return send(src, dst, at(0, 1), not_right, not_left)

    def send_left(src, dst):
        return send(src, dst, at(0, -1), not_left, not_right)

    def arrived(name, copies):
        with jax.named_scope("await_" + name):
            for copy, comes in copies:
                if comes is None:
                    copy.wait_recv()
                else:
                    pl.when(comes)(copy.wait_recv)

    not_top, not_bottom = tx > 0, tx < NTX - 1
    not_left, not_right = ty > 0, ty < NTY - 1

    def keep(flag, value):
        return jnp.where(flag, value, 0.0)

    for copy in bring[:3]:
        copy.wait()
    decoder = (seg >= NSEG // 2).astype(F32)
    encoder = 1.0 - decoder

    def iota(shape, axis):
        return lax.broadcasted_iota(jnp.int32, shape, axis)

    orow = nown[...].astype(F32)
    crow = ncell[...].astype(F32)
    n0, n1 = iota((CELLS, CELLS), 0), iota((CELLS, CELLS), 1)
    ocol = jnp.sum(jnp.where(n0 == n1, orow, 0.0), axis=1, keepdims=True)
    ccol = jnp.sum(jnp.where(n0 == n1, crow, 0.0), axis=1, keepdims=True)
    same = jnp.where(ocol == orow, 1.0, 0.0)
    slot_row = jnp.sum(jnp.where(n0 < n1, same, 0.0), axis=0, keepdims=True)
    slot_col = jnp.sum(jnp.where(n1 < n0, same, 0.0), axis=1, keepdims=True)
    tyf = ty.astype(F32)

    def place(owner, slots):
        offset = owner - tyf
        return jnp.where(offset < 0.0, offset + NTY, offset) * CAP + slots

    qrow, qcol = place(orow, slot_row), place(ocol, slot_col)
    chosen = jnp.where(iota((NTY * CAP, CELLS), 0).astype(F32) == qrow, 1.0, 0.0).astype(BF)
    cell_hot = jnp.where(ccol == iota((CELLS, 128), 1).astype(F32), 1.0, 0.0).astype(BF)
    asked = dot(chosen, cell_hot)
    for q in range(NTY):
        rqs[q] = asked[q * CAP : (q + 1) * CAP].astype(BF)
    rqr[0] = rqs[0]

    for copy in bring[3:6]:
        copy.wait()
    spread = iota((WT, WT // 4), 1) == (iota((WT, WT // 4), 0) >> 2)
    for k in range(HT // 4):
        row = land[k : k + 1, :].astype(F32)
        weight = jnp.sum(jnp.where(spread, row, 0.0), axis=1, keepdims=True)
        weight = jnp.where(seg == NSEG - 1, weight, 1.0)
        for y in range(4 * k, 4 * k + 4):
            part = pl.ds(y * WT, WT)
            value = (gra[part, :].astype(F32) + encoder * par[part, :].astype(F32)) * weight
            g32[part, :] = value.astype(BF).astype(F32)
    t32[...] = sta[...].astype(F32)

    last = (HT - 1) * WT
    srow_s[0] = sta[last : last + WT, :]
    srow_s[1] = g32[last : last + WT, :].astype(BF)
    ogup_s[...] = g32[0:WT, :].astype(BF)
    colr_s[0] = t32[pl.ds(WT - 1, HT, stride=WT), :].astype(BF)
    colr_s[1] = g32[pl.ds(WT - 1, HT, stride=WT), :].astype(BF)
    coll_s[...] = g32[pl.ds(0, HT, stride=WT), :].astype(BF)

    with jax.named_scope("await_entry"):
        pl.semaphore_wait(barrier, len(greeted))

    request = [send(rqs.at[q], rqr.at[q], ty_peer(q)) for q in range(1, NTY)]
    rim_tx = [
        send(srow_s, top_r, at(1, 0)),
        send(ogup_s, bot_r, at(-1, 0)),
        send(colr_s, ctl_r, at(1, 1)),
        send(coll_s, ctr_r, at(1, -1)),
        send(colr_s.at[1], cbl_r, at(-1, 1)),
        send(coll_s, cbr_r, at(-1, -1)),
    ]
    rim_ty = [send_right(colr_s, lft_r), send_left(coll_s, rgt_r)]

    for copy in bring[6:]:
        copy.wait()
    dwp[C2:CP, :] = jnp.zeros((CP - C2, 9 * C), BF)
    for t in range(9):
        dwp[0:C2, t * C : (t + 1) * C] = dw[t]
    uc[C2:CP, :] = jnp.zeros((CP - C2, 16 * C), BF)
    for u in range(4):
        for v in range(4):
            total = None
            for a in TAPS_OF[u]:
                for b in TAPS_OF[v]:
                    tap = uw[a * 3 + b].astype(F32)
                    total = tap if total is None else total + tap
            block = (u * 4 + v) * C
            uc[0:C2, block : block + C] = total.astype(BF)

    def fill(oo, ee, fine):
        ee[1:17, 0:W2, :] = fine[pl.ds(0, HT * W2, stride=2), :].reshape(HT, W2, C)
        oo[1:17, 8:40, :] = fine[pl.ds(1, HT * W2, stride=2), :].reshape(HT, W2, C)

    def fill_row(oo, ee, r, flag, row):
        tr[...] = keep(flag, row.astype(F32))
        ee[r, 0:W2, :] = tr[pl.ds(0, W2, stride=2), :]
        oo[r, 8:40, :] = tr[pl.ds(1, W2, stride=2), :]

    def fill_col(plane, first, at_col, flag, column):
        values = keep(flag, column.astype(F32))
        for r in range(values.shape[0]):
            plane[first + r, at_col : at_col + 1, :] = values[r : r + 1, :]

    def fill_cell(plane, r, at_col, flag, column, i):
        values = keep(flag, column.astype(F32))
        plane[r, at_col : at_col + 1, :] = values[i : i + 1, :]

    def half_col(j):
        halves = [r32[h, pl.ds(j, H2, stride=W2), :] for h in range(2)]
        return jnp.concatenate(halves, axis=1).astype(BF)

    def gather_down(oo, ee, first, n, lhs, row):
        span = slice(2 * first, 2 * first + 2 * n + 2)
        for b, view in enumerate([oo[span, 7:39, :], ee[span, 0:32, :], oo[span, 8:40, :]]):
            pairs = view.astype(BF).reshape(n + 1, 2, W2, C)
            for a in range(3):
                block = (a * 3 + b) * C
                part = pairs[a // 2 : a // 2 + n, a % 2].reshape(n * W2, C)
                lhs[row : row + n * W2, block : block + C] = part

    fill(soo, see, t32)
    fill(goo, gee, g32)

    def gather_wide(first, n, lhs, row):
        span = slice(2 * first, 2 * first + 2 * n + 2)
        views = [goo[span, 7:39, :], gee[span, 0:32, :], goo[span, 8:40, :], gee[span, 1:33, :]]
        for v, view in enumerate(views):
            pairs = view.astype(BF).reshape(n + 1, 2, W2, C)
            for u in range(4):
                block = (u * 4 + v) * C
                part = pairs[u // 2 : u // 2 + n, u % 2].reshape(n * W2, C)
                lhs[row : row + n * W2, block : block + C] = part

    def backward(narrow, wide):
        pre_back = dot(narrow[...], dwp[...], ((1,), (1,)))
        gate = jax.nn.sigmoid(pre_back)
        raised = (pre_back * gate).astype(BF)
        pooled = dot(wide[...], uc[...], ((1,), (1,)))
        pre_grad = (pooled * (gate * (1.0 + pre_back * (1.0 - gate)))).astype(BF)
        down_part = dot(narrow[...], pre_grad, ((0,), (0,)))
        up_part = dot(raised, wide[...], ((0,), (0,)))
        return pre_grad.astype(F32), down_part, up_part

    def put_half(value, row):
        r32[0, row : row + value.shape[0], :] = value[:, 0:C]
        r32[1, row : row + value.shape[0], :] = value[:, C:CP]

    arrived("rim_ty", rim_ty)
    fill_col(soo, 1, 7, not_left, lft_r[0])
    fill_col(goo, 1, 7, not_left, lft_r[1])
    fill_col(gee, 1, W2, not_right, rgt_r[...])
    gather_down(soo, see, 1, H2 - 2, dim, 0)
    gather_wide(1, H2 - 2, wim, 0)
    inner, down_part, up_part = backward(dim, wim)
    put_half(inner, W2)
    pgf[1 : H2 - 1, 0:W2, :] = inner.reshape(H2 - 2, W2, CP)
    gds[0] = down_part[:, 0:C]
    gds[1] = down_part[:, C:CP]
    pw[...] = up_part

    arrived("request", request)
    wanted = jnp.concatenate([rqr[q].astype(F32) for q in range(NTY)], axis=0)
    answer = dot(wanted[:, 0:CELLS].astype(BF), coarse[...])
    for q in range(NTY):
        rps[q] = answer[q * CAP : (q + 1) * CAP].astype(BF)
    rpr[0] = rps[0]
    reply = [
        send(rps.at[q], rpr.at[q], (seg, tx, lax.rem(ty + NTY - q, NTY))) for q in range(1, NTY)
    ]

    arrived("rim_tx", rim_tx)
    fill_row(soo, see, 0, not_top, top_r[0])
    fill_row(goo, gee, 0, not_top, top_r[1])
    fill_row(goo, gee, 17, not_bottom, bot_r[...])
    fill_cell(soo, 0, 7, not_top & not_left, ctl_r[0], HT - 1)
    fill_cell(goo, 0, 7, not_top & not_left, ctl_r[1], HT - 1)
    fill_cell(gee, 0, W2, not_top & not_right, ctr_r[...], HT - 1)
    fill_cell(goo, 17, 7, not_bottom & not_left, cbl_r[...], 0)
    fill_cell(gee, 17, W2, not_bottom & not_right, cbr_r[...], 0)
    for first, row in ((0, 0), (H2 - 1, W2)):
        gather_down(soo, see, first, 1, dimg, row)
        gather_wide(first, 1, wimg, row)
    outer, down_part, up_part = backward(dimg, wimg)
    put_half(outer[0:W2], 0)
    put_half(outer[W2:], M2 - W2)
    pgrow_s[...] = outer[0:W2].astype(BF)
    pgcol_s[...] = half_col(0)
    pg_rim = [
        send(pgrow_s, pgrow_r, at(-1, 0)),
        send(pgcol_s, pgcor_r, at(-1, -1)),
        send_left(pgcol_s, pgcol_r),
    ]
    pgf[0, 0:W2, :] = outer[0:W2]
    pgf[H2 - 1, 0:W2, :] = outer[W2:]
    gds[0] = gds[0] + down_part[:, 0:C]
    gds[1] = gds[1] + down_part[:, C:CP]
    pw[...] = pw[...] + up_part

    low = iota((ROWS // 3, C), 1) < 64
    even_lo = gds[0, pl.ds(0, ROWS // 3, stride=2), :]
    even_hi = gds[1, pl.ds(0, ROWS // 3, stride=2), :]
    odd_lo = pltpu.roll(gds[0, pl.ds(1, ROWS // 3, stride=2), :], 64, 1)
    odd_hi = pltpu.roll(gds[1, pl.ds(1, ROWS // 3, stride=2), :], 64, 1)
    gf[0, pl.ds(0, ROWS // 3, stride=3), :] = even_lo
    gf[0, pl.ds(1, ROWS // 3, stride=3), :] = jnp.where(low, even_hi, odd_lo)
    gf[0, pl.ds(2, ROWS // 3, stride=3), :] = jnp.where(low, odd_lo, odd_hi)
    for a in range(3):
        for b in range(3):
            total = None
            for u in (2 - a, 3 - a):
                for v in (2 - b, 3 - b):
                    block = (u * 4 + v) * C
                    term = pw[0:C2, block : block + C]
                    total = term if total is None else total + term
            tap = (a * 3 + b) * C2
            gf[1, tap : tap + C2, :] = total
    gb[...] = gf[1 - core].astype(BF)
    swap = send(gb, ra, sibling)

    arrived("swap", [swap])
    gs[...] = gf[core] + ra[...].astype(F32)
    yb[...] = gs[...].astype(BF).reshape(NY, QUART, C)
    y_sum = [send(yb.at[lax.rem(yy + q, NY)], ry.at[q - 1], y_peer(q)) for q in (2, 1, 3)]

    arrived("reply", reply)
    table = jnp.concatenate([rpr[q].astype(F32) for q in range(NTY)], axis=0).astype(BF)
    pick = jnp.where(iota((CELLS, NTY * CAP), 1).astype(F32) == qcol, 1.0, 0.0).astype(BF)
    fetched = dot(pick, table).astype(BF)
    r0, r1 = iota((4 * WT, CELLS), 0), iota((4 * WT, CELLS), 1)
    widen = jnp.where(r1 == ((r0 >> 6) << 4) + ((r0 & 63) >> 2), 1.0, 0.0).astype(BF)
    condb[...] = dot(widen, fetched)
    for y in range(HT):
        part = pl.ds(y * WT, WT)
        value = (
            act[part, :].astype(F32)
            + decoder * par[part, :].astype(F32)
            + condb[pl.ds(y // 4 * WT, WT), :]
        )
        b32[part, :] = value.astype(BF).astype(F32)
    birow_s[...] = b32[last : last + WT, :].astype(BF)
    bicol_s[...] = b32[pl.ds(WT - 1, HT, stride=WT), :].astype(BF)
    biup_s[...] = b32[0 : 2 * WT, :].astype(BF)
    bi_tx = [
        send(birow_s, birow_r, at(1, 0)),
        send(biup_s, biup_r, at(-1, 0)),
        send(bicol_s, bicor_r, at(1, 1)),
        send(bicol_s, bibl_r, at(-1, 1)),
    ]
    bi_ty = [send_right(bicol_s, bicol_r)]
    fill(boo, bee, b32)

    def reduce(lhs):
        pre_down = dot(lhs[...], dwp[...], ((1,), (1,)))
        return (pre_down * jax.nn.sigmoid(pre_down)).astype(BF).astype(F32)

    arrived("bi_ty", bi_ty)
    fill_col(boo, 1, 7, not_left, bicol_r[...])
    gather_down(boo, bee, 1, H2 - 1, dimf, 0)
    half_grid = reduce(dimf)
    r32[0, W2:M2, :] = half_grid[:, 0:C]
    r32[1, W2:M2, :] = half_grid[:, C:CP]
    rdb_s[...] = half_grid[M2 - 2 * W2 :].astype(BF)
    rdl_s[...] = half_col(0)
    rdr_s[...] = half_col(W2 - 1)
    red_tx = [
        send(rdb_s, rdt_r, at(1, 0)),
        send(rdr_s, rtl_r, at(1, 1)),
        send(rdl_s, rtr_r, at(1, -1)),
    ]
    red_ty = [send_right(rdr_s, rdl_r), send_left(rdl_s, rdr_r)]
    rpf[2 : H2 + 1, 8:40, :] = half_grid.reshape(H2 - 1, W2, CP)

    parts = [pl.ds(3 * WT, 12 * WT), pl.ds(0, 3 * WT), pl.ds(15 * WT, WT)]
    slots = [(slot(), slot()) for _ in parts]

    def block_copies(source):
        return [
            (make(up, source.at[part, :], left_out.at[part, :], seg_next),
             make(down, source.at[part, :], right_out.at[part, :], seg_prev))
            for part, (up, down) in zip(parts, slots)
        ]

    ig_copies, out_copies = block_copies(pay_ig), block_copies(pay_out)

    def send_output(which):
        @pl.when(seg <= NSEG - 2)
        def _():
            for k in which:
                out_copies[k][0].start()

        @pl.when(seg == 0)
        def _():
            for k in which:
                out_copies[k][1].start()

    arrived("red_ty", red_ty)
    fill_col(rpf, 1, 7, not_left, rdl_r[...])
    fill_col(rpf, 1, 40, not_right, rdr_r[...])
    meets = (((0, 3), (1, 1)), ((1, 2), (2, 0)))

    def output_rows(pr, first, n):
        for pc in range(2):
            span = slice(2 * first + pr + 1, 2 * first + pr + 1 + 2 * n)
            plane = bee[span, 0:32, :] if pc == 0 else boo[span, 8:40, :]
            value = plane.reshape(n, 2, W2, C)[:, 0].reshape(n * W2, C)
            for di, u in meets[pr]:
                for dj, v in meets[pc]:
                    block = (u * 4 + v) * C
                    lhs = rpf[first + di : first + di + n, 7 + dj : 39 + dj, :]
                    lhs = lhs.astype(BF).reshape(n * W2, CP)
                    value = value + dot(lhs, uc[:, block : block + C])
            for k in range(n):
                start = (2 * (first + k) + pr) * WT + pc
                t32[pl.ds(start, W2, stride=2), :] = value[k * W2 : (k + 1) * W2]

    output_rows(0, 2, 6)
    output_rows(1, 1, 6)
    pay_out[3 * WT : 15 * WT, :] = t32[3 * WT : 15 * WT, :].astype(BF)
    send_output((0,))
    arrived("y_sum", y_sum)
    total = gs[pl.ds(yy * QUART, QUART), :]
    for q in range(NY - 1):
        total = total + ry[q].astype(F32)
    zs[0:QUART, :] = total
    zs[QUART:, :] = jnp.zeros((zs.shape[0] - QUART, C), F32)
    for z in range(NZ):
        zp[z] = zs[z * PIECE : z * PIECE + PADP, :]
    zb[...] = zp[...].astype(BF)
    z_sum = [send(zb.at[lax.rem(zz + q, NZ)], rz.at[q - 1], z_peer(q)) for q in FAR_FIRST]
    arrived("pg_rim", pg_rim)
    pgf[H2, 0:W2, :] = keep(not_bottom, pgrow_r[...].astype(F32))
    fill_col(pgf, 0, W2, not_right, pgcol_r[...])
    fill_cell(pgf, H2, W2, not_bottom & not_right, pgcor_r[...], 0)
    shifted = [
        [pgf[di : di + H2, dj : dj + W2, :].astype(BF).reshape(M2, CP) for dj in (0, 1)]
        for di in (0, 1)
    ]

    def spread_out(value, pr, pc):
        for i in range(H2):
            t32[pl.ds((2 * i + pr) * WT + pc, W2, stride=2), :] = value[i * W2 : (i + 1) * W2]

    for pr in range(2):
        for pc in range(2):
            plane = gee[:, 0:32, :] if pc == 0 else goo[:, 8:40, :]
            value = rows_of(plane, 1 + pr)
            for a, di in ((1, 0),) if pr == 0 else ((2, 0), (0, 1)):
                for b, dj in ((1, 0),) if pc == 0 else ((2, 0), (0, 1)):
                    tap = (a * 3 + b) * C
                    value = value + dot(shifted[di][dj], dwp[:, tap : tap + C])
            spread_out(value, pr, pc)
    pay_ig[...] = t32[...].astype(BF)

    @pl.when(seg == NSEG - 1)
    def _():
        for copy, _ in ig_copies:
            copy.start()

    @pl.when(seg >= 1)
    def _():
        for _, copy in ig_copies:
            copy.start()

    arrived("bi_tx", bi_tx)
    fill_row(boo, bee, 0, not_top, birow_r[...])
    fill_cell(boo, 0, 7, not_top & not_left, bicor_r[...], HT - 1)
    for k in range(2):
        fill_row(boo, bee, 17 + k, not_bottom, biup_r[k * WT : (k + 1) * WT, :])
        fill_cell(boo, 17 + k, 7, not_bottom & not_left, bibl_r[...], k)
    gather_down(boo, bee, 0, 1, dimh, 0)
    gather_down(boo, bee, H2, 1, dimh, W2)
    half_grid = reduce(dimh)
    upper = iota((8, CP), 0) == 0
    rel_s[...] = jnp.where(upper, half_grid[0:1], half_grid[W2 : W2 + 1]).astype(BF)
    rer_s[...] = jnp.where(upper, half_grid[W2 - 1 : W2], half_grid[2 * W2 - 1 :]).astype(BF)
    red_late = [send_right(rer_s, rel_r), send_left(rel_s, rer_r)]
    rpf[1, 8:40, :] = half_grid[0:W2]
    rpf[H2 + 1, 8:40, :] = keep(not_bottom, half_grid[W2:])

    arrived("red_tx", red_tx)
    rpf[0, 8:40, :] = keep(not_top, rdt_r[...].astype(F32))
    fill_cell(rpf, 0, 7, not_top & not_left, rtl_r[...], H2 - 1)
    fill_cell(rpf, 0, 40, not_top & not_right, rtr_r[...], H2 - 1)
    arrived("red_late", red_late)
    for column, flag, got in ((7, not_left, rel_r), (40, not_right, rer_r)):
        fill_cell(rpf, 1, column, flag, got[...], 0)
        fill_cell(rpf, H2 + 1, column, flag & not_bottom, got[...], 1)
    output_rows(0, 0, 2)
    output_rows(1, 0, 1)
    output_rows(1, H2 - 1, 1)
    pay_out[0 : 3 * WT, :] = t32[0 : 3 * WT, :].astype(BF)
    pay_out[15 * WT :, :] = t32[15 * WT :, :].astype(BF)
    send_output((1, 2))

    arrived("z_sum", z_sum)
    total = zp[zz]
    for q in range(NZ - 1):
        total = total + rz[q].astype(F32)
    scaling = 1.0 / math.sqrt(HT * WT * NTX * NTY)
    fin[...] = total * scaling
    last_swap = send(fin, rfin, sibling)
    arrived("last_swap", [last_swap])
    mine, other = fin[...], rfin[...]
    first = core == 0
    head = iota((16, C), 1) < 64
    for out, value in ((down_out, jnp.where(first, mine, other)), (up_out, jnp.where(first, other, mine))):
        fs[...] = pltpu.roll(value, 64, 1)
        second_half = jnp.where(head, fs[13:29, :], fs[14:30, :])
        half = jnp.where(first, value[0:16], second_half)
        for r in range(13):
            out[0:1, r * C : (r + 1) * C] = half[r : r + 1, :]
        out[0:1, 13 * C : 13 * C + 64] = half[13:14, 0:64]

    with jax.named_scope("await_blocks"):
        for pair in out_copies:
            for copy in pair:
                copy.wait_recv()
    for pair in out_copies:
        for copy in pair:
            copy.wait_send()
    for copy, goes in started:
        if goes is None:
            copy.wait_send()
        else:
            pl.when(goes)(copy.wait_send)


def finish(left_h, right_h, down_h, up_h, act_o, grad_o, partner_o, down_o, up_o,
           left, right, down, up, blank, isem, osem):
    seg = lax.axis_index("segment")
    even = lax.rem(seg, 2) == 0
    bring = [
        pltpu.make_async_copy(src, dst, isem.at[i])
        for i, (src, dst) in enumerate(((left_h, left), (right_h, right), (down_h, down), (up_h, up)))
    ]
    for copy in bring:
        copy.start()

    @pl.when((seg == 0) | (seg == NSEG - 1))
    def _():
        blank[...] = jnp.zeros_like(blank)

    ends = [
        pltpu.make_async_copy(left, act_o, osem.at[0]),
        pltpu.make_async_copy(right, grad_o, osem.at[1]),
        pltpu.make_async_copy(left, partner_o, osem.at[2]),
        pltpu.make_async_copy(down, down_o, osem.at[3]),
        pltpu.make_async_copy(up, up_o, osem.at[4]),
    ]

    @pl.when(seg == 0)
    def _():
        pltpu.make_async_copy(blank, act_o, osem.at[0]).start()

    @pl.when(seg == NSEG - 1)
    def _():
        pltpu.make_async_copy(blank, grad_o, osem.at[1]).start()

    for copy in bring:
        copy.wait()

    @pl.when(seg > 0)
    def _():
        ends[0].start()

    @pl.when(seg < NSEG - 1)
    def _():
        ends[1].start()

    @pl.when(even)
    def _():
        ends[2].start()

    @pl.when(jnp.logical_not(even))
    def _():
        pltpu.make_async_copy(right, partner_o, osem.at[2]).start()

    ends[3].start()
    ends[4].start()
    for copy in ends:
        copy.wait()


N_COPIES = 15 + 8 + 15 + 3 + 1 + 3 + 5 + 6 + 5 + 15 + 2 + 1


def whole_step(act, par, sta, gra, dw, uw, coarse, nown, ncell, land):
    vm = pltpu.VMEM
    fine_rows = HT * WT
    scratch = [
        vm((fine_rows, C), BF), vm((fine_rows, C), BF), vm((fine_rows, C), BF), vm((fine_rows, C), BF),
        vm((9, C2, C), BF), vm((9, C2, C), BF), vm((CELLS, C), BF), vm((1, CELLS), jnp.int32),
        vm((1, CELLS), jnp.int32), vm((HT // 4, WT // 4), jnp.int32),
        vm((CP, 9 * C), BF), vm((CP, 16 * C), BF), vm((fine_rows, C), F32), vm((fine_rows, C), F32),
        vm((fine_rows, C), F32),
        vm((18, 40, C), F32), vm((18, 40, C), F32), vm((18, 40, C), F32), vm((18, 40, C), F32),
        vm((20, 40, C), F32), vm((20, 40, C), F32),
        vm((M2 - 2 * W2, 9 * C), BF), vm((M2 - W2, 9 * C), BF), vm((2 * W2, 9 * C), BF),
        vm((2 * W2, 9 * C), BF), vm((M2 - 2 * W2, 16 * C), BF), vm((2 * W2, 16 * C), BF),
        vm((H2 + 1, 40, CP), F32), vm((H2 + 2, 48, CP), F32), vm((2, M2, C), F32),
        vm((CP, 16 * C), F32), vm((2, 9 * C, C), F32), vm((2, ROWS, C), F32), vm((ROWS, C), F32),
        vm((448, C), F32), vm((NZ, PADP, C), F32), vm((PADP, C), F32),
        vm((fine_rows, C), BF), vm((fine_rows, C), BF),
        vm((NTY, CAP, 128), BF), vm((NTY, CAP, 128), BF), vm((NTY, CAP, C), BF), vm((NTY, CAP, C), BF),
        vm((4 * WT, C), F32), vm((WT, C), F32),
        vm((2, WT, C), BF), vm((WT, C), BF), vm((2, HT, C), BF), vm((HT, C), BF),
        vm((2, WT, C), BF), vm((WT, C), BF), vm((2, HT, C), BF), vm((HT, C), BF),
        vm((2, HT, C), BF), vm((HT, C), BF), vm((HT, C), BF), vm((HT, C), BF),
        vm((W2, CP), BF), vm((H2, CP), BF), vm((W2, CP), BF), vm((H2, CP), BF), vm((H2, CP), BF),
        vm((WT, C), BF), vm((2 * WT, C), BF), vm((HT, C), BF),
        vm((WT, C), BF), vm((2 * WT, C), BF), vm((HT, C), BF), vm((HT, C), BF), vm((HT, C), BF),
        vm((W2, CP), BF), vm((H2, CP), BF), vm((H2, CP), BF), vm((8, CP), BF), vm((8, CP), BF),
        vm((W2, CP), BF), vm((H2, CP), BF), vm((H2, CP), BF), vm((H2, CP), BF), vm((H2, CP), BF),
        vm((8, CP), BF), vm((8, CP), BF),
        vm((ROWS, C), BF), vm((ROWS, C), BF), vm((NY, QUART, C), BF), vm((NY - 1, QUART, C), BF),
        vm((NZ, PADP, C), BF), vm((NZ - 1, PADP, C), BF), vm((PADP, C), F32), vm((PADP, C), F32),
        pltpu.SemaphoreType.DMA((N_COPIES,)), pltpu.SemaphoreType.DMA((N_COPIES,)),
        pltpu.SemaphoreType.DMA((10,)),
    ]
    in_vmem = pl.BlockSpec(memory_space=pltpu.VMEM)
    return pl.pallas_call(
        kernel,
        out_shape=(
            jax.ShapeDtypeStruct((fine_rows, C), BF),
            jax.ShapeDtypeStruct((fine_rows, C), BF),
            jax.ShapeDtypeStruct((1, ROWS), F32),
            jax.ShapeDtypeStruct((1, ROWS), F32),
        ),
        in_specs=[pl.BlockSpec(memory_space=pl.ANY)] * 10,
        out_specs=(
            pl.BlockSpec(memory_space=pl.ANY), pl.BlockSpec(memory_space=pl.ANY), in_vmem, in_vmem,
        ),
        scratch_shapes=scratch,
        compiler_params=pltpu.CompilerParams(
            collective_id=0, has_side_effects=True, vmem_limit_bytes=56 << 20
        ),
        name="relay",
    )(act, par, sta, gra, dw, uw, coarse, nown, ncell, land)


def local(
    act_in, partner_in, stashed, grad_in, down_weights, up_weights, coarse, nest_owner, nest_cell,
    land_weight,
):
    flat = (HT * WT, C)
    from_before, from_after, down_sum, up_sum = whole_step(
        act_in.reshape(flat), partner_in.reshape(flat), stashed.reshape(flat), grad_in.reshape(flat),
        jnp.swapaxes(down_weights, 3, 4).reshape(9, C2, C), up_weights.reshape(9, C2, C), coarse,
        nest_owner.reshape(1, CELLS),
        nest_cell.reshape(1, CELLS), land_weight,
    )
    block = jax.ShapeDtypeStruct(flat, BF)
    sums = jax.ShapeDtypeStruct((1, ROWS), F32)
    anywhere = pl.BlockSpec(memory_space=pl.ANY)
    act_out, grad_out, partner_out, down_sum, up_sum = pl.pallas_call(
        finish,
        out_shape=(block, block, block, sums, sums),
        in_specs=[anywhere] * 4,
        out_specs=(anywhere,) * 5,
        scratch_shapes=[
            pltpu.VMEM(flat, BF), pltpu.VMEM(flat, BF), pltpu.VMEM((1, ROWS), F32),
            pltpu.VMEM((1, ROWS), F32), pltpu.VMEM(flat, BF),
            pltpu.SemaphoreType.DMA((4,)), pltpu.SemaphoreType.DMA((5,)),
        ],
        name="finish",
    )(from_before, from_after, down_sum, up_sum)
    tile = (1, HT, WT, C)
    return (
        act_out.reshape(tile), grad_out.reshape(tile), partner_out.reshape(tile), down_sum, up_sum,
    )


def solution(mesh):
    placed = (
        P("segment", "tx", "ty", None),
        P("segment", "tx", "ty", None),
        P("segment", "tx", "ty", None),
        P("segment", "tx", "ty", None),
        P("segment", None, None, None, None),
        P("segment", None, None, None, None),
        P(("tx", "ty"), None),
        P(("tx", "ty"), None),
        P(("tx", "ty")),
        P("tx", "ty"),
    )
    return jax.shard_map(
        local,
        mesh=mesh,
        in_specs=placed,
        out_specs=(
            P("segment", "tx", "ty", None),
            P("segment", "tx", "ty", None),
            P("segment", "tx", "ty", None),
            P("segment", ("tx", "ty")),
            P("segment", ("tx", "ty")),
        ),
        check_vma=False,
    )
```
